256 devices in a mesh: freq: 32 (over z, x), panel: 8 (over y, core).
Axes of the slice: x: 4, y: 4, z: 8, core: 2. Of those that a mesh axis runs over, the one named last changes fastest.
Arguments:
- wavefield: float32 [32, 2, 128, 8192], P('freq', None, None, 'panel'), may hold values from -6 to 6
- direct: float32 [32, 2, 128, 8192], P('freq', None, None, 'panel'), may hold values from -6 to 6
- left_factors: float32 [32, 8192, 6, 128], P('freq', 'panel'), may hold values from -0.375 to 0.375
- right_factors: float32 [32, 32, 6, 256, 128], P('freq', 'panel'), may hold values from -0.3125 to 0.3125
- tile_src: int32 [32, 6], P('panel'), may hold values from -1 to 7, as said below
- onset: int32 [128, 2048], P('freq'), may hold values from 128 to 895
Outputs:
- focusing: float32 [32, 2, 128, 8192], P('freq', None, None, 'panel')
The draws below stay inside these ranges and needn't reach their ends.
Inputs may be any that keep to these rules, and one draw needn't show every extreme that they name: `tile_src`: in each receiver panel's row the first k slots name distinct source tiles, with 2 <= k <= 6, and the other slots hold -1; in every aligned block of 4 panels at least one panel fills all 6 slots.
All inputs are finite; a program needn't handle non-finite values.
Results may differ from the reference program's by a relative error of at most 0.0003.
Values sent between devices are 32-bit elements; how exact they have to be, the bound alone decides.
No kernel may reach another device: no remote copies, remote signals or barrier semaphores. Data moves between devices by JAX's collectives and lax.ppermute only.
A program may use at most 128 MiB of HBM per device.

```python
import math
import jax
import jax.numpy as jnp
from jax import lax

TILE = 256
RANK = 64
SRC_TILES = 8
SLOTS = 6
VS = 128
NT = 1024
FIRST_BIN = 8
RP_DEV = 4
PANELS = 32
RECV = 8192
SRC = 2048
NF = 32


def draw_tile_src(key, part):
    key_order = jax.random.fold_in(key, 11)
    key_count = jax.random.fold_in(key, 23)
    key_full = jax.random.fold_in(key, 37)
    scores = jax.random.randint(key_order, (PANELS, SRC_TILES), 0, 1 << 20) * SRC_TILES + jnp.arange(SRC_TILES, dtype=jnp.int32)[None, :]
    order = jnp.argsort(scores, axis=1).astype(jnp.int32)[:, :SLOTS]
    counts = jax.random.randint(key_count, (PANELS,), 2, SLOTS + 1)
    full_at = jax.random.randint(key_full, (PANELS // RP_DEV,), 0, RP_DEV)
    position = jnp.arange(PANELS, dtype=jnp.int32) % RP_DEV
    counts = jnp.where(position == jnp.repeat(full_at, RP_DEV), SLOTS, counts)
    slot_index = jnp.arange(SLOTS, dtype=jnp.int32)
    return jnp.where(slot_index[None, :] < counts[:, None], order, -1).astype(jnp.int32)


def set_ends(values, own_key, smallest, top_value):
    extent = values.shape
    index_at = [jax.random.randint(jax.random.fold_in(own_key, axis), (), 0, extent[axis]) for axis in range(len(extent))]
    values = values.at[tuple(index_at)].set(smallest)
    longest = extent.index(max(extent))
    index_at[longest] = (index_at[longest] + 1) % extent[longest]
    return values.at[tuple(index_at)].set(top_value)


def shard_levels(rng, shape, pieces, least, top_value):
    factor_of, own = 1.0, jax.random.fold_in(rng, 6)
    for dim, blocks in pieces:
        draws = jnp.exp(jax.random.uniform(jax.random.fold_in(own, dim), (blocks,), jnp.float32, least / len(pieces), top_value / len(pieces)))
        factor_of = factor_of * jnp.repeat(draws, shape[dim] // blocks).reshape([-1 if axis == dim else 1 for axis in range(len(shape))])
    return factor_of


def centred(own_key, shape, spread, most, pieces=(), kind=jnp.bfloat16):
    drawn = spread * jax.random.normal(own_key, shape, jnp.float32)
    if pieces:
        drawn = drawn * shard_levels(own_key, shape, pieces, -0.22, 0.18)
    return jnp.clip(drawn, -most, most).astype(kind)


def setup_inputs(seed: int = 0) -> dict:
    key_of = jax.random.split(jax.random.key(seed), 7)
    wavefield = centred(key_of[0], (NF, 2, VS, RECV), 1.0, 6.0, ((0, 32), (3, 8)), jnp.float32)
    direct = centred(key_of[1], (NF, 2, VS, RECV), 1.0, 6.0, ((0, 32), (3, 8)), jnp.float32)
    left_factors = centred(key_of[2], (NF, RECV, SLOTS, 2 * RANK), TILE ** -0.5, 0.375, ((0, 32), (1, 8)), jnp.float32)
    right_factors = centred(key_of[3], (NF, PANELS, SLOTS, TILE, 2 * RANK), (RANK * SLOTS) ** -0.5, 0.3125, ((0, 32), (1, 8)), jnp.float32)
    tile_src = draw_tile_src(jax.random.fold_in(key_of[6], 71), 0)
    onset = set_ends(jax.random.randint(key_of[5], (VS, SRC), NT // 8, NT - NT // 8), jax.random.fold_in(key_of[5], 1), NT // 8, (NT - NT // 8) - 1).astype(jnp.int32)
    return {"wavefield": wavefield, "direct": direct, "left_factors": left_factors, "right_factors": right_factors, "tile_src": tile_src, "onset": onset}


HIGH = lax.Precision.HIGHEST

def pair_coef(products):
    half = products.shape[3] // 2
    real_part = products[0, :, :, :half] + products[1, :, :, half:]
    imag_part = products[1, :, :, :half] - products[0, :, :, half:]
    return jnp.stack([jnp.concatenate([real_part, -imag_part], axis=2), jnp.concatenate([imag_part, real_part], axis=2)])

def tile_adjoint(left, right, field, picks):
    products = jnp.einsum('ptsk,cvpt->cpskv', left, field, precision=HIGH)
    contrib = jnp.einsum('pstk,cpskv->cpstv', right, pair_coef(products), precision=HIGH)
    return jnp.einsum('psj,cpstv->cvjt', picks, contrib, precision=HIGH)

def tile_forward(left, right, source_field, picks):
    chosen = jnp.einsum('psj,cvjt->cpsvt', picks, source_field, precision=HIGH)
    products = jnp.einsum('pstk,cpsvt->cpskv', right, chosen, precision=HIGH)
    return jnp.einsum('ptsk,cpskv->cvpt', left, pair_coef(products), precision=HIGH)

def time_tables(count, length):
    times = jnp.arange(length, dtype=jnp.int32)
    freqs = jnp.arange(count, dtype=jnp.int32) + FIRST_BIN
    phase = freqs[None, :] * times[:, None] % length
    angle = 2.0 * math.pi / length * phase.astype(jnp.float32)
    waves = jnp.stack([jnp.cos(angle), -jnp.sin(angle)], axis=2).reshape(length, 2 * count)
    return (waves * (1.0 / math.sqrt(count)), waves.T * (1.0 / math.sqrt(length)))

def gate_block(block, marks, into, outof):
    count = block.shape[0]
    width = block.shape[2]
    length = into.shape[0]
    traces = jnp.dot(into, block.reshape(2 * count, width), precision=HIGH, preferred_element_type=jnp.float32)
    times = jnp.arange(length, dtype=jnp.int32)
    gated = jnp.where(times[:, None] < marks[None, :], traces, jnp.zeros_like(traces))
    back = jnp.dot(outof, gated, precision=HIGH, preferred_element_type=jnp.float32)
    return back.reshape(count, 2, width)

def apply_gate(moved, marks, into, outof):
    items = jnp.moveaxis(moved, 2, 0)
    result = lax.map(lambda pair: gate_block(pair[0], pair[1], into, outof), (items, marks))
    return jnp.moveaxis(result, 0, 2)

def reference(wavefield, direct, left_factors, right_factors, tile_src, onset):
    picks = (tile_src[:, :, None] == jnp.arange(SRC_TILES, dtype=jnp.int32)[None, None, :]).astype(jnp.float32)

    def adjoint_one(args):
        field, left, right = args
        left4 = left.reshape(PANELS, TILE, SLOTS, 2 * RANK)
        field4 = field.reshape(2, VS, PANELS, TILE)
        return tile_adjoint(left4, right, field4, picks).reshape(2, VS, SRC)
    adjoint = lax.map(adjoint_one, (wavefield, left_factors, right_factors))
    into, outof = time_tables(NF, NT)
    back = apply_gate(adjoint, onset, into, outof)

    def forward_one(args):
        source_field, left, right = args
        left4 = left.reshape(PANELS, TILE, SLOTS, 2 * RANK)
        result = tile_forward(left4, right, source_field.reshape(2, VS, SRC_TILES, TILE), picks)
        return result.reshape(2, VS, RECV)
    forward = lax.map(forward_one, (back, left_factors, right_factors))
    return direct - forward
```

```python
import math

import jax
import jax.numpy as jnp
import ml_dtypes
import numpy as np
from jax import lax
from jax.experimental import pallas as pl
from jax.experimental.pallas import tpu as pltpu
from jax.sharding import PartitionSpec as P

NT = 1024
FIRST_BIN = 8
T_USED = 896

F32 = jnp.float32
BF16 = jnp.bfloat16
NN = (((1,), (0,)), ((), ()))
NT_DIMS = (((1,), (1,)), ((), ()))


def split(x):
    high = x.astype(BF16)
    low = (x - high.astype(F32)).astype(BF16)
    return high, low


def dot(a, b, dims=NN):
    return lax.dot_general(a, b, dims, preferred_element_type=F32)


def pair_coef(products, rank):
    half = products.shape[0] // 2
    real, imag = products[:half], products[half:]
    lane = lax.broadcasted_iota(jnp.int32, real.shape, 1)
    sign = jnp.where(lane < rank, 1.0, -1.0).astype(F32)
    first = real + sign * pltpu.roll(imag, rank, 1)
    second = imag - sign * pltpu.roll(real, rank, 1)
    return jnp.concatenate([first, second], axis=0)


def adjoint_kernel(src_ref, me_ref, field_ref, left_ref, right_ref, own_ref, other_ref):
    p = pl.program_id(0)
    slots, tile, width = left_ref.shape
    rank = width // 2
    me = me_ref[0]

    @pl.when(p == 0)
    def _():
        own_ref[...] = jnp.zeros_like(own_ref)
        other_ref[...] = jnp.zeros_like(other_ref)

    field = field_ref[...]
    field_h, field_l = split(field.reshape(field.shape[0] * field.shape[1], tile))
    for s in range(0, slots, 2):
        left_h, left_l = split(jnp.concatenate([left_ref[s], left_ref[s + 1]], axis=1))
        both = dot(field_h, left_h) + dot(field_l, left_h) + dot(field_h, left_l)
        for k in range(2):
            target = src_ref[p, s + k]

            @pl.when(target >= 0)
            def _():
                coef_h, coef_l = split(pair_coef(both[:, k * width : (k + 1) * width], rank))
                right_h, right_l = split(right_ref[0, s + k])
                value = dot(
                    jnp.concatenate([coef_h, coef_l], axis=1),
                    jnp.concatenate([right_h, right_h], axis=1),
                    NT_DIMS,
                ) + dot(coef_h, right_l, NT_DIMS)
                step = lax.rem(target // 2 - me // 2 + 4, 4)
                mine = lax.rem(target, 2) == lax.rem(me, 2)

                @pl.when(mine)
                def _():
                    own_ref[step] += value

                @pl.when(jnp.logical_not(mine))
                def _():
                    other_ref[step] += value


def sum_kernel(a_ref, b_ref, c_ref, d_ref, out_ref):
    total = (a_ref[...] + b_ref[...]) + (c_ref[...] + d_ref[...])
    rows, cols = total.shape
    lanes = cols // 2
    half = total.reshape(2, rows // 16, 8, cols)
    for c in range(2):
        left, right = half[c, :, :, :lanes], half[c, :, :, lanes:]
        low = lax.broadcasted_iota(jnp.int32, left.shape, 1) < 4
        even = jnp.where(low, left, pltpu.roll(right, 4, 1))
        odd = jnp.where(low, pltpu.roll(left, 4, 1), right)
        out_ref[:, 8 * c : 8 * c + 8, :] = jnp.stack([even, odd], axis=1).reshape(rows // 8, 8, lanes)


def gate_kernel(me_ref, x_ref, onset_ref, into_ref, outof_ref, y_ref):
    group = onset_ref.shape[0]
    lanes = x_ref.shape[1]
    bands = outof_ref.shape[0] // 2
    for v in range(group):
        picks = [pl.ds(h * group + v, bands, stride=2 * group) for h in range(2)]
        high, low = split(jnp.concatenate([x_ref[pick, :] for pick in picks], axis=1))
        traces = dot(into_ref[...], jnp.concatenate([high, high, low], axis=0))
        when = lax.broadcasted_iota(jnp.int32, traces.shape, 0)
        gated = jnp.where(when < onset_ref[v : v + 1, :], traces, 0.0)
        high, low = split(gated)
        pair = dot(outof_ref[...], high)
        back = pair[:bands] + pair[bands:] + dot(outof_ref[:bands, :], low)
        for h in range(2):
            y_ref[picks[h], :] = back[:, h * lanes : (h + 1) * lanes]


def forward_kernel(src_ref, me_ref, *refs):
    tile_refs, (left_ref, right_ref, direct_ref, out_ref, high_ref, low_ref, coef_h, coef_l) = refs[:8], refs[8:]
    p = pl.program_id(0)
    slots, tile, width = left_ref.shape
    rank = width // 2
    me = me_ref[0]

    @pl.when(p == 0)
    def _():
        for i in range(8):
            count, _, lanes = tile_refs[i].shape
            block = tile_refs[i][...].reshape(count // 2, 2, 2, 8, lanes)
            parts = []
            for c in range(2):
                even, odd = block[:, 0, c], block[:, 1, c]
                low = lax.broadcasted_iota(jnp.int32, even.shape, 1) < 4
                first = jnp.where(low, even, pltpu.roll(odd, 4, 1)).reshape(count * 4, lanes)
                second = jnp.where(low, pltpu.roll(even, 4, 1), odd).reshape(count * 4, lanes)
                parts.append(jnp.concatenate([first, second], axis=1))
            h, l = split(jnp.concatenate(parts, axis=0))
            high_ref[i] = h
            low_ref[i] = l

    for s in range(slots):
        source = src_ref[p, s]
        lanes = slice(s * width, (s + 1) * width)

        @pl.when(source >= 0)
        def _():
            step = lax.rem(source // 2 - me // 2 + 4, 4)
            place = step + jnp.where(lax.rem(source, 2) == lax.rem(me, 2), 0, 4)
            right_h, right_l = split(right_ref[0, s])
            high = high_ref[place]
            pair = dot(high, jnp.concatenate([right_h, right_l], axis=1))
            products = pair[:, :width] + pair[:, width:] + dot(low_ref[place], right_h)
            h, l = split(pair_coef(products, rank))
            coef_h[:, lanes] = h
            coef_l[:, lanes] = l

        @pl.when(source < 0)
        def _():
            coef_h[:, lanes] = jnp.zeros((coef_h.shape[0], width), BF16)
            coef_l[:, lanes] = jnp.zeros((coef_l.shape[0], width), BF16)

    left_h, left_l = split(jnp.concatenate([left_ref[s] for s in range(slots)], axis=1))
    high = coef_h[...]
    result = dot(high, left_h, NT_DIMS) + dot(coef_l[...], left_h, NT_DIMS) + dot(high, left_l, NT_DIMS)
    out_ref[...] = direct_ref[...] - result.reshape(out_ref.shape)


def time_tables(count):
    times = np.arange(T_USED, dtype=np.int64)
    phase = (np.arange(count, dtype=np.int64) + FIRST_BIN)[None, :] * times[:, None] % NT
    angle = 2.0 * math.pi / NT * phase
    waves = np.stack([np.cos(angle), -np.sin(angle)], axis=2).reshape(T_USED, 2 * count)

    def parts(x):
        high = x.astype(ml_dtypes.bfloat16)
        return high, (x - high.astype(np.float64)).astype(ml_dtypes.bfloat16)

    high, low = parts(waves / math.sqrt(count))
    into = np.concatenate([high, low, high], axis=1)
    high, low = parts(waves.T / math.sqrt(NT))
    return into, np.concatenate([high, low], axis=0)


def shards(wavefield, direct, left_factors, right_factors, tile_src, onset):
    panels, slots = tile_src.shape
    tile, width = right_factors.shape[3:]
    virtual = wavefield.shape[2]
    rows = 2 * virtual
    mib = 1024 * 1024
    left = jnp.transpose(left_factors[0], (1, 0, 2))
    right = right_factors[0]
    me = lax.axis_index("panel").astype(jnp.int32)[None]
    count = lax.axis_size("freq")
    group = virtual // count

    left_spec = pl.BlockSpec((slots, tile, width), lambda p, *_: (0, p, 0))
    right_spec = pl.BlockSpec((1, slots, tile, width), lambda p, *_: (p, 0, 0, 0))
    field_spec = pl.BlockSpec((2, virtual, tile), lambda p, *_: (0, 0, p))
    sums_spec = pl.BlockSpec((4, rows, tile), lambda p, *_: (0, 0, 0))
    sums_type = jax.ShapeDtypeStruct((4, rows, tile), F32)
    own, other = pl.pallas_call(
        adjoint_kernel,
        grid_spec=pltpu.PrefetchScalarGridSpec(
            num_scalar_prefetch=2,
            grid=(panels,),
            in_specs=[field_spec, left_spec, right_spec],
            out_specs=[sums_spec, sums_spec],
        ),
        out_shape=[sums_type, sums_type],
        compiler_params=pltpu.CompilerParams(vmem_limit_bytes=20 * mib),
        name="adjoint",
    )(tile_src, me, wavefield[0], left, right)

    swap = [(i, i ^ 1) for i in range(8)]

    def shift(x, by):
        return lax.ppermute(x, "panel", [(i, (i + 2 * by) % 8) for i in range(8)])

    summed = own + lax.ppermute(other, "panel", swap)
    parts = [summed[0]] + [shift(summed[b], b) for b in range(1, 4)]
    moved = pl.pallas_call(
        sum_kernel,
        out_shape=jax.ShapeDtypeStruct((count, 4 * group, tile // 2), F32),
        compiler_params=pltpu.CompilerParams(vmem_limit_bytes=4 * mib),
        name="panel_sum",
    )(*parts)
    moved = lax.all_to_all(moved, "freq", split_axis=0, concat_axis=0, tiled=True)

    into, outof = time_tables(count)
    whole = lambda shape: pl.BlockSpec(shape, lambda i, *_: (0,) * len(shape))
    gated = pl.pallas_call(
        gate_kernel,
        grid_spec=pltpu.PrefetchScalarGridSpec(
            num_scalar_prefetch=1,
            grid=(1,),
            in_specs=[
                whole((2 * rows, tile // 2)),
                pl.BlockSpec((group, tile), lambda i, me_ref: (0, me_ref[0])),
                whole(into.shape),
                whole(outof.shape),
            ],
            out_specs=whole((2 * rows, tile // 2)),
        ),
        out_shape=jax.ShapeDtypeStruct((2 * rows, tile // 2), F32),
        compiler_params=pltpu.CompilerParams(vmem_limit_bytes=12 * mib),
        name="gate",
    )(me, moved.reshape(2 * rows, tile // 2), onset, jnp.asarray(into), jnp.asarray(outof))
    back = lax.all_to_all(gated.reshape(count, 4 * group, tile // 2), "freq", split_axis=0, concat_axis=0, tiled=True)

    tiles = [back] + [shift(back, -b) for b in range(1, 4)]
    tiles = tiles + [lax.ppermute(t, "panel", swap) for t in tiles]
    tile_spec = whole((count, 4 * group, tile // 2))
    return pl.pallas_call(
        forward_kernel,
        grid_spec=pltpu.PrefetchScalarGridSpec(
            num_scalar_prefetch=2,
            grid=(panels,),
            in_specs=[tile_spec] * 8 + [left_spec, right_spec, field_spec],
            out_specs=field_spec,
            scratch_shapes=[
                pltpu.VMEM((8, rows, tile), BF16),
                pltpu.VMEM((8, rows, tile), BF16),
                pltpu.VMEM((rows, slots * width), BF16),
                pltpu.VMEM((rows, slots * width), BF16),
            ],
        ),
        out_shape=jax.ShapeDtypeStruct(direct.shape[1:], F32),
        compiler_params=pltpu.CompilerParams(vmem_limit_bytes=24 * mib),
        name="forward",
    )(tile_src, me, *tiles, left, right, direct[0])[None]


def solution(mesh):
    in_specs = (
        P("freq", None, None, "panel"),
        P("freq", None, None, "panel"),
        P("freq", "panel", None, None),
        P("freq", "panel", None, None, None),
        P("panel", None),
        P("freq", None),
    )
    out_specs = P("freq", None, None, "panel")
    return jax.shard_map(shards, mesh=mesh, in_specs=in_specs, out_specs=out_specs, check_vma=False)
```

```python
import functools
import math

import jax
import jax.numpy as jnp
import ml_dtypes
import numpy as np
from jax import lax
from jax.experimental import pallas as pl
from jax.experimental.pallas import tpu as pltpu
from jax.sharding import PartitionSpec as P

NT = 1024
FIRST_BIN = 8
T_USED = 896

F32 = jnp.float32
BF16 = jnp.bfloat16
NN = (((1,), (0,)), ((), ()))
NT_DIMS = (((1,), (1,)), ((), ()))


def split(x):
    high = x.astype(BF16)
    low = (x - high.astype(F32)).astype(BF16)
    return high, low


def dot(a, b, dims=NN):
    return lax.dot_general(a, b, dims, preferred_element_type=F32)


def pair_coef(products, rank):
    half = products.shape[0] // 2
    real, imag = products[:half], products[half:]
    lane = lax.broadcasted_iota(jnp.int32, real.shape, 1)
    sign = jnp.where(lane < rank, 1.0, -1.0).astype(F32)
    first = real + sign * pltpu.roll(imag, rank, 1)
    second = imag - sign * pltpu.roll(real, rank, 1)
    return jnp.concatenate([first, second], axis=0)


def find_slot(src_ref, panel, target, slots):
    slot, found = jnp.int32(0), jnp.int32(0)
    for s in range(slots):
        hit = src_ref[panel, s] == target
        slot = jnp.where(hit, s, slot)
        found = jnp.where(hit, 1, found)
    return slot, jnp.where(found > 0, panel * slots + slot, src_ref.shape[0] * slots)


def tile_of(me, step, other):
    return lax.rem(me // 2 + step, 4) * 2 + lax.rem(me + other, 2)


def spread(src_ref, me, other, coef_h, coef_l, right_ref, out_ref):
    width = coef_h.shape[2]
    for step in range(out_ref.shape[0]):
        target = tile_of(me, step, other)
        parts = []
        for p in range(src_ref.shape[0]):
            _, at = find_slot(src_ref, p, target, src_ref.shape[1])
            parts.append((coef_h[at], coef_l[at], right_ref[at, :, :width], right_ref[at, :, width:]))
        high, low, right_h, right_l = (jnp.concatenate(x, axis=1) for x in zip(*parts))
        out_ref[step] = dot(high, right_h, NT_DIMS) + dot(low, right_h, NT_DIMS) + dot(high, right_l, NT_DIMS)


def adjoint_kernel(
    me_ref, src_hbm, field_hbm, left_hbm, right_hbm,
    coef_h, coef_l, right_ref, left_ref, out_ref,
    src_ref, field_ref, raw_ref, sems,
):
    panels, slots, tile, width = left_ref.shape
    copies = []
    for p in range(panels):
        at = pl.ds(p * tile, tile)
        copies.append(
            (
                pltpu.make_async_copy(field_hbm.at[:, :, at], field_ref.at[p], sems.at[0, p]),
                pltpu.make_async_copy(left_hbm.at[:, at, :], left_ref.at[p], sems.at[1, p]),
            )
        )
    rights = [pltpu.make_async_copy(right_hbm.at[p], raw_ref.at[p], sems.at[2, p]) for p in range(panels)]
    names = pltpu.make_async_copy(src_hbm, src_ref, sems.at[3, 0])
    for pair in copies:
        pair[0].start()
        pair[1].start()
    for copy in rights:
        copy.start()
    names.start()
    last = panels * slots
    coef_h[last] = jnp.zeros(coef_h.shape[1:], BF16)
    coef_l[last] = jnp.zeros(coef_l.shape[1:], BF16)
    right_ref[last] = jnp.zeros(right_ref.shape[1:], BF16)
    for p in range(panels):
        copies[p][0].wait()
        copies[p][1].wait()
        field_h, field_l = split(field_ref[p].reshape(-1, tile))
        for s in range(0, slots, 2):
            left_h, left_l = split(jnp.concatenate([left_ref[p, s], left_ref[p, s + 1]], axis=1))
            both = dot(field_h, left_h) + dot(field_l, left_h) + dot(field_h, left_l)
            for k in range(2):
                high, low = split(pair_coef(both[:, k * width : (k + 1) * width], width // 2))
                coef_h[p * slots + s + k] = high
                coef_l[p * slots + s + k] = low
    for p in range(panels):
        rights[p].wait()
        for s in range(slots):
            right_ref[p * slots + s] = jnp.concatenate(split(raw_ref[p, s]), axis=1)
    names.wait()
    spread(src_ref, me_ref[0], 1, coef_h, coef_l, right_ref, out_ref)


def own_kernel(src_ref, me_ref, coef_h, coef_l, right_ref, left_ref, out_ref, left_h, left_l):
    spread(src_ref, me_ref[0], 0, coef_h, coef_l, right_ref, out_ref)
    for p in range(left_ref.shape[0]):
        for s in range(left_ref.shape[1]):
            left_h[p, s], left_l[p, s] = split(left_ref[p, s])


def sum_kernel(a_ref, b_ref, c_ref, d_ref, out_ref):
    total = (a_ref[...] + b_ref[...]) + (c_ref[...] + d_ref[...])
    rows, cols = total.shape
    lanes = cols // 2
    half = total.reshape(2, rows // 16, 8, cols)
    for c in range(2):
        left, right = half[c, :, :, :lanes], half[c, :, :, lanes:]
        low = lax.broadcasted_iota(jnp.int32, left.shape, 1) < 4
        even = jnp.where(low, left, pltpu.roll(right, 4, 1))
        odd = jnp.where(low, pltpu.roll(left, 4, 1), right)
        out_ref[:, 8 * c : 8 * c + 8, :] = jnp.stack([even, odd], axis=1).reshape(rows // 8, 8, lanes)


def gate_kernel(me_ref, x_ref, onset_ref, into_ref, outof_ref, y_ref):
    group = onset_ref.shape[0]
    lanes = x_ref.shape[1]
    bands = outof_ref.shape[0] // 2
    for v in range(group):
        picks = [pl.ds(h * group + v, bands, stride=2 * group) for h in range(2)]
        high, low = split(jnp.concatenate([x_ref[pick, :] for pick in picks], axis=1))
        traces = dot(into_ref[...], jnp.concatenate([high, high, low], axis=0))
        when = lax.broadcasted_iota(jnp.int32, traces.shape, 0)
        gated = jnp.where(when < onset_ref[v : v + 1, :], traces, 0.0)
        high, low = split(gated)
        pair = dot(outof_ref[...], high)
        back = pair[:bands] + pair[bands:] + dot(outof_ref[:bands, :], low)
        for h in range(2):
            y_ref[picks[h], :] = back[:, h * lanes : (h + 1) * lanes]


def forward_kernel(step, last, src_ref, me_ref, own_ref, other_ref, left_h, left_l, right_ref, total_ref, out_ref, *scratch):
    panels, slots, tile, width = left_h.shape
    me = me_ref[0]
    tiles = []
    for ref in (own_ref, other_ref):
        count, _, lanes = ref.shape
        block = ref[...].reshape(count // 2, 2, 2, 8, lanes)
        parts = []
        for c in range(2):
            even, odd = block[:, 0, c], block[:, 1, c]
            low = lax.broadcasted_iota(jnp.int32, even.shape, 1) < 4
            first = jnp.where(low, even, pltpu.roll(odd, 4, 1)).reshape(count * 4, lanes)
            second = jnp.where(low, pltpu.roll(even, 4, 1), odd).reshape(count * 4, lanes)
            parts.append(jnp.concatenate([first, second], axis=1))
        tiles.append(split(jnp.concatenate(parts, axis=0)))
    copies = []
    for p in range(panels):
        at = slice(p * tile, (p + 1) * tile)
        parts = []
        for i, (high, low) in enumerate(tiles):
            slot, place = find_slot(src_ref, p, tile_of(me, step, i), slots)
            right = right_ref[place]
            pair = dot(high, right)
            products = pair[:, :width] + pair[:, width:] + dot(low, right[:, :width])
            parts.append(split(pair_coef(products, width // 2)) + (left_h[p, slot], left_l[p, slot]))
        high, low, there_h, there_l = (jnp.concatenate(x, axis=1) for x in zip(*parts))
        result = dot(high, there_h, NT_DIMS) + dot(low, there_h, NT_DIMS) + dot(high, there_l, NT_DIMS)
        result = total_ref[:, :, at] - result.reshape(total_ref.shape[0], total_ref.shape[1], tile)
        if last:
            kept, sems = scratch
            kept[p] = result
            copies.append(pltpu.make_async_copy(kept.at[p], out_ref.at[:, :, pl.ds(p * tile, tile)], sems.at[p]))
            copies[p].start()
        else:
            out_ref[:, :, at] = result
    for copy in copies:
        copy.wait()


def time_tables(count):
    times = np.arange(T_USED, dtype=np.int64)
    phase = (np.arange(count, dtype=np.int64) + FIRST_BIN)[None, :] * times[:, None] % NT
    angle = 2.0 * math.pi / NT * phase
    waves = np.stack([np.cos(angle), -np.sin(angle)], axis=2).reshape(T_USED, 2 * count)

    def parts(x):
        high = x.astype(ml_dtypes.bfloat16)
        return high, (x - high.astype(np.float64)).astype(ml_dtypes.bfloat16)

    high, low = parts(waves / math.sqrt(count))
    into = np.concatenate([high, low, high], axis=1)
    high, low = parts(waves.T / math.sqrt(NT))
    return into, np.concatenate([high, low], axis=0)


def shards(wavefield, direct, left_factors, right_factors, tile_src, onset):
    panels, slots = tile_src.shape
    tile, width = right_factors.shape[3:]
    virtual = wavefield.shape[2]
    rows = 2 * virtual
    mib = 1024 * 1024
    left = jnp.transpose(left_factors[0], (1, 0, 2))
    right = right_factors[0]
    me = lax.axis_index("panel").astype(jnp.int32)[None]
    count = lax.axis_size("freq")
    group = virtual // count

    in_vmem = pl.BlockSpec(memory_space=pltpu.VMEM)
    in_smem = pl.BlockSpec(memory_space=pltpu.SMEM)
    in_hbm = pl.BlockSpec(memory_space=pltpu.HBM)
    hbm = lambda x: pltpu.with_memory_space_constraint(x, pltpu.HBM)
    sums_type = jax.ShapeDtypeStruct((4, rows, tile), F32)
    places = panels * slots + 1
    cost = pl.CostEstimate(flops=3_000_000_000, bytes_accessed=8_000_000, transcendentals=0)
    coef_type = jax.ShapeDtypeStruct((places, rows, width), BF16)
    left_shape = (panels, slots, tile, width)
    coef_h, coef_l, right_kept, left_kept, other = pl.pallas_call(
        adjoint_kernel,
        in_specs=[in_smem] + [in_hbm] * 4,
        out_specs=[in_vmem] * 5,
        out_shape=[
            coef_type,
            coef_type,
            jax.ShapeDtypeStruct((places, tile, 2 * width), BF16),
            jax.ShapeDtypeStruct(left_shape, F32),
            sums_type,
        ],
        scratch_shapes=[
            pltpu.SMEM(tile_src.shape, jnp.int32),
            pltpu.VMEM((panels, 2, virtual, tile), F32),
            pltpu.VMEM((panels, slots, tile, width), F32),
            pltpu.SemaphoreType.DMA((4, panels)),
        ],
        compiler_params=pltpu.CompilerParams(vmem_limit_bytes=28 * mib),
        name="adjoint",
    )(me, hbm(tile_src), hbm(wavefield[0]), hbm(left), hbm(right))
    own, left_h, left_l = pl.pallas_call(
        own_kernel,
        in_specs=[in_smem, in_smem] + [in_vmem] * 4,
        out_specs=[in_vmem] * 3,
        out_shape=[sums_type, jax.ShapeDtypeStruct(left_shape, BF16), jax.ShapeDtypeStruct(left_shape, BF16)],
        compiler_params=pltpu.CompilerParams(vmem_limit_bytes=24 * mib),
        cost_estimate=cost,
        name="own",
    )(tile_src, me, coef_h, coef_l, right_kept, left_kept)

    swap = [(i, i ^ 1) for i in range(8)]

    def shift(x, by):
        return lax.ppermute(x, "panel", [(i, (i + 2 * by) % 8) for i in range(8)])

    summed = own + lax.ppermute(other, "panel", swap)
    parts = [summed[0]] + [shift(summed[b], b) for b in range(1, 4)]
    moved = pl.pallas_call(
        sum_kernel,
        out_shape=jax.ShapeDtypeStruct((count, 4 * group, tile // 2), F32),
        compiler_params=pltpu.CompilerParams(vmem_limit_bytes=4 * mib),
        name="panel_sum",
    )(*parts)
    moved = lax.all_to_all(moved, "freq", split_axis=0, concat_axis=0, tiled=True)

    into, outof = time_tables(count)
    whole = lambda shape: pl.BlockSpec(shape, lambda i, *_: (0,) * len(shape))
    gated = pl.pallas_call(
        gate_kernel,
        grid_spec=pltpu.PrefetchScalarGridSpec(
            num_scalar_prefetch=1,
            grid=(1,),
            in_specs=[
                whole((2 * rows, tile // 2)),
                pl.BlockSpec((group, tile), lambda i, me_ref: (0, me_ref[0])),
                whole(into.shape),
                whole(outof.shape),
            ],
            out_specs=whole((2 * rows, tile // 2)),
        ),
        out_shape=jax.ShapeDtypeStruct((2 * rows, tile // 2), F32),
        compiler_params=pltpu.CompilerParams(vmem_limit_bytes=12 * mib),
        name="gate",
    )(me, moved.reshape(2 * rows, tile // 2), onset, jnp.asarray(into), jnp.asarray(outof))
    back = lax.all_to_all(gated.reshape(count, 4 * group, tile // 2), "freq", split_axis=0, concat_axis=0, tiled=True)

    def exchange(x):
        return lax.ppermute(x, "panel", swap)

    def forward(step, mine, theirs, total, last=False):
        return pl.pallas_call(
            functools.partial(forward_kernel, step, last),
            in_specs=[in_smem, in_smem] + [in_vmem] * 6,
            out_specs=in_hbm if last else in_vmem,
            out_shape=jax.ShapeDtypeStruct(total.shape, F32),
            scratch_shapes=[pltpu.VMEM((panels, 2, virtual, tile), F32), pltpu.SemaphoreType.DMA((panels,))] if last else [],
            compiler_params=pltpu.CompilerParams(vmem_limit_bytes=22 * mib),
            cost_estimate=cost,
            name=f"forward_{step}",
        )(tile_src, me, mine, theirs, left_h, left_l, right_kept, total)

    mine = {step: shift(back, -step) for step in (1, 3, 2)}
    total = forward(0, back, exchange(back), direct[0])
    mine[1], mine[3], total = lax.optimization_barrier((mine[1], mine[3], total))
    theirs = {step: exchange(mine[step]) for step in (1, 3)}
    total = forward(1, mine[1], theirs[1], total)
    mine[2], total = lax.optimization_barrier((mine[2], total))
    theirs[2] = exchange(mine[2])
    total = forward(3, mine[3], theirs[3], total)
    return forward(2, mine[2], theirs[2], total, last=True)[None]


def solution(mesh):
    in_specs = (
        P("freq", None, None, "panel"),
        P("freq", None, None, "panel"),
        P("freq", "panel", None, None),
        P("freq", "panel", None, None, None),
        P("panel", None),
        P("freq", None),
    )
    out_specs = P("freq", None, None, "panel")
    return jax.shard_map(shards, mesh=mesh, in_specs=in_specs, out_specs=out_specs, check_vma=False)
```

```python
import functools
import math

import jax
import jax.numpy as jnp
import ml_dtypes
import numpy as np
from jax import lax
from jax.experimental import pallas as pl
from jax.experimental.pallas import tpu as pltpu
from jax.sharding import PartitionSpec as P

NT = 1024
FIRST_BIN = 8
T_USED = 896

F32 = jnp.float32
BF16 = jnp.bfloat16
NN = (((1,), (0,)), ((), ()))
NT_DIMS = (((1,), (1,)), ((), ()))
AWAY = (2, 1, 3)


def split(x):
    high = x.astype(BF16)
    low = (x - high.astype(F32)).astype(BF16)
    return high, low


def dot(a, b, dims=NN):
    return lax.dot_general(a, b, dims, preferred_element_type=F32)


def pair_coef(products, rank):
    half = products.shape[0] // 2
    real, imag = products[:half], products[half:]
    lane = lax.broadcasted_iota(jnp.int32, real.shape, 1)
    sign = jnp.where(lane < rank, 1.0, -1.0).astype(F32)
    first = real + sign * pltpu.roll(imag, rank, 1)
    second = imag - sign * pltpu.roll(real, rank, 1)
    return jnp.concatenate([first, second], axis=0)


def find_slot(src_ref, panel, target, slots):
    slot, found = jnp.int32(0), jnp.int32(0)
    for s in range(slots):
        hit = src_ref[panel, s] == target
        slot = jnp.where(hit, s, slot)
        found = jnp.where(hit, 1, found)
    return slot, jnp.where(found > 0, panel * slots + slot, src_ref.shape[0] * slots)


def tile_of(me, step, other):
    return lax.rem(me // 2 + step, 4) * 2 + lax.rem(me + other, 2)


def spread(src_ref, me, targets, coef_h, coef_l, right_ref, out_ref):
    width = coef_h.shape[2]
    for i, (step, other) in enumerate(targets):
        target = tile_of(me, step, other)
        parts = []
        for p in range(src_ref.shape[0]):
            _, at = find_slot(src_ref, p, target, src_ref.shape[1])
            parts.append((coef_h[at], coef_l[at], right_ref[at, :, :width], right_ref[at, :, width:]))
        high, low, right_h, right_l = (jnp.concatenate(x, axis=1) for x in zip(*parts))
        out_ref[i] = dot(high, right_h, NT_DIMS) + dot(low, right_h, NT_DIMS) + dot(high, right_l, NT_DIMS)


def adjoint_kernel(
    me_ref, src_hbm, field_hbm, left_hbm, right_hbm,
    coef_h, coef_l, right_ref, left_ref, out_ref,
    src_ref, field_ref, raw_ref, sems,
):
    panels, slots, tile, width = left_ref.shape
    copies = []
    for p in range(panels):
        at = pl.ds(p * tile, tile)
        copies.append(
            (
                pltpu.make_async_copy(field_hbm.at[:, :, at], field_ref.at[p], sems.at[0, p]),
                pltpu.make_async_copy(left_hbm.at[:, at, :], left_ref.at[p], sems.at[1, p]),
            )
        )
    rights = [pltpu.make_async_copy(right_hbm.at[p], raw_ref.at[p], sems.at[2, p]) for p in range(panels)]
    names = pltpu.make_async_copy(src_hbm, src_ref, sems.at[3, 0])
    for pair in copies[:2]:
        pair[0].start()
        pair[1].start()
    last = panels * slots
    coef_h[last] = jnp.zeros(coef_h.shape[1:], BF16)
    coef_l[last] = jnp.zeros(coef_l.shape[1:], BF16)
    right_ref[last] = jnp.zeros(right_ref.shape[1:], BF16)
    for p in range(panels):
        copies[p][0].wait()
        copies[p][1].wait()
        if p + 2 < panels:
            copies[p + 2][0].start()
            copies[p + 2][1].start()
        elif p + 2 == panels:
            names.start()
            for copy in rights:
                copy.start()
        field_h, field_l = split(field_ref[p].reshape(-1, tile))
        for s in range(0, slots, 2):
            left_h, left_l = split(jnp.concatenate([left_ref[p, s], left_ref[p, s + 1]], axis=1))
            both = dot(field_h, left_h) + dot(field_l, left_h) + dot(field_h, left_l)
            for k in range(2):
                high, low = split(pair_coef(both[:, k * width : (k + 1) * width], width // 2))
                coef_h[p * slots + s + k] = high
                coef_l[p * slots + s + k] = low
    for p in range(panels):
        rights[p].wait()
        for s in range(slots):
            right_ref[p * slots + s] = jnp.concatenate(split(raw_ref[p, s]), axis=1)
    names.wait()
    spread(src_ref, me_ref[0], [(step, 1) for step in AWAY], coef_h, coef_l, right_ref, out_ref)


def own_kernel(src_ref, me_ref, coef_h, coef_l, right_ref, out_ref):
    spread(src_ref, me_ref[0], [(step, 0) for step in AWAY], coef_h, coef_l, right_ref, out_ref)


def here_kernel(src_ref, me_ref, coef_h, coef_l, right_ref, left_ref, _, out_ref, left_h, left_l):
    spread(src_ref, me_ref[0], [(0, 1), (0, 0)], coef_h, coef_l, right_ref, out_ref)
    for p in range(left_ref.shape[0]):
        for s in range(left_ref.shape[1]):
            left_h[p, s], left_l[p, s] = split(left_ref[p, s])


def chip_sum_kernel(own_ref, swapped_ref, up_ref, down_ref, up_half, down_half):
    half = up_half.shape[0]
    up_ref[0] = own_ref[0, :half] + swapped_ref[0, :half]
    down_ref[0] = own_ref[0, half:] + swapped_ref[0, half:]
    up_half[...] = own_ref[1, :half] + swapped_ref[1, :half]
    up_ref[1] = own_ref[1, half:] + swapped_ref[1, half:]
    down_ref[1] = own_ref[2, :half] + swapped_ref[2, :half]
    down_half[...] = own_ref[2, half:] + swapped_ref[2, half:]


def relay_kernel(up_half, from_below, down_half, from_above, up_ref, down_ref):
    up_ref[...] = up_half[...] + from_below[0]
    down_ref[...] = down_half[...] + from_above[0]


def sum_kernel(here_ref, swapped_ref, below, above, relayed_below, relayed_above, out_ref):
    totals = (
        (here_ref[1, : relayed_below.shape[0]] + swapped_ref[: relayed_below.shape[0]])
        + (relayed_below[...] + above[1]),
        (here_ref[1, relayed_below.shape[0] :] + swapped_ref[relayed_below.shape[0] :])
        + (relayed_above[...] + below[1]),
    )
    for c, total in enumerate(totals):
        rows, cols = total.shape
        lanes = cols // 2
        block = total.reshape(rows // 8, 8, cols)
        left, right = block[:, :, :lanes], block[:, :, lanes:]
        low = lax.broadcasted_iota(jnp.int32, left.shape, 1) < 4
        even = jnp.where(low, left, pltpu.roll(right, 4, 1))
        odd = jnp.where(low, pltpu.roll(left, 4, 1), right)
        out_ref[:, 8 * c : 8 * c + 8, :] = jnp.stack([even, odd], axis=1).reshape(rows // 4, 8, lanes)


def gate_kernel(_, me_ref, x_ref, onset_ref, into_ref, outof_ref, y_ref):
    group = onset_ref.shape[0]
    lanes = x_ref.shape[1]
    here = pl.ds(pl.multiple_of(me_ref[0] * (2 * lanes), 2 * lanes), 2 * lanes)
    bands = outof_ref.shape[0] // 2
    for v in range(group):
        picks = [pl.ds(h * group + v, bands, stride=2 * group) for h in range(2)]
        high, low = split(jnp.concatenate([x_ref[pick, :] for pick in picks], axis=1))
        traces = dot(into_ref[...], jnp.concatenate([high, high, low], axis=0))
        when = lax.broadcasted_iota(jnp.int32, traces.shape, 0)
        gated = jnp.where(when < onset_ref[v : v + 1, here], traces, 0.0)
        high, low = split(gated)
        pair = dot(outof_ref[...], high)
        back = pair[:bands] + pair[bands:] + dot(outof_ref[:bands, :], low)
        for h in range(2):
            y_ref[picks[h], :] = back[:, h * lanes : (h + 1) * lanes]


def forward_kernel(steps, last, pieces, src_ref, me_ref, *refs):
    number = 2 * len(steps)
    left_h, left_l, right_ref, total_ref, out_ref, *scratch = refs[number * pieces :]
    panels, slots, tile, width = left_h.shape
    me = me_ref[0]
    tiles = []
    for i in range(number):
        got = jnp.concatenate([ref[...] for ref in refs[i * pieces : (i + 1) * pieces]], axis=0)
        count, _, lanes = got.shape
        block = got.reshape(count // 2, 2, 2, 8, lanes)
        parts = []
        for c in range(2):
            even, odd = block[:, 0, c], block[:, 1, c]
            low = lax.broadcasted_iota(jnp.int32, even.shape, 1) < 4
            first = jnp.where(low, even, pltpu.roll(odd, 4, 1)).reshape(count * 4, lanes)
            second = jnp.where(low, pltpu.roll(even, 4, 1), odd).reshape(count * 4, lanes)
            parts.append(jnp.concatenate([first, second], axis=1))
        tiles.append(split(jnp.concatenate(parts, axis=0)))
    copies = []
    for p in range(panels):
        at = slice(p * tile, (p + 1) * tile)
        parts = []
        for i, (high, low) in enumerate(tiles):
            slot, place = find_slot(src_ref, p, tile_of(me, steps[i // 2], i % 2), slots)
            right = right_ref[place]
            pair = dot(high, right)
            products = pair[:, :width] + pair[:, width:] + dot(low, right[:, :width])
            parts.append(split(pair_coef(products, width // 2)) + (left_h[p, slot], left_l[p, slot]))
        high, low, there_h, there_l = (jnp.concatenate(x, axis=1) for x in zip(*parts))
        result = dot(high, there_h, NT_DIMS) + dot(low, there_h, NT_DIMS) + dot(high, there_l, NT_DIMS)
        result = total_ref[:, :, at] - result.reshape(total_ref.shape[0], total_ref.shape[1], tile)
        if last:
            kept, sems = scratch
            kept[p] = result
            copies.append(pltpu.make_async_copy(kept.at[p], out_ref.at[:, :, pl.ds(p * tile, tile)], sems.at[p]))
            copies[p].start()
        else:
            out_ref[:, :, at] = result
    for copy in copies:
        copy.wait()


def time_tables(count):
    times = np.arange(T_USED, dtype=np.int64)
    phase = (np.arange(count, dtype=np.int64) + FIRST_BIN)[None, :] * times[:, None] % NT
    angle = 2.0 * math.pi / NT * phase
    waves = np.stack([np.cos(angle), -np.sin(angle)], axis=2).reshape(T_USED, 2 * count)

    def parts(x):
        high = x.astype(ml_dtypes.bfloat16)
        return high, (x - high.astype(np.float64)).astype(ml_dtypes.bfloat16)

    high, low = parts(waves / math.sqrt(count))
    into = np.concatenate([high, low, high], axis=1)
    high, low = parts(waves.T / math.sqrt(NT))
    return into, np.concatenate([high, low], axis=0)


def shards(wavefield, direct, left_factors, right_factors, tile_src, onset):
    panels, slots = tile_src.shape
    tile, width = right_factors.shape[3:]
    virtual = wavefield.shape[2]
    rows = 2 * virtual
    mib = 1024 * 1024
    left = jnp.transpose(left_factors[0], (1, 0, 2))
    right = right_factors[0]
    me = lax.axis_index("panel").astype(jnp.int32)[None]
    count = lax.axis_size("freq")
    group = virtual // count

    in_vmem = pl.BlockSpec(memory_space=pltpu.VMEM)
    in_smem = pl.BlockSpec(memory_space=pltpu.SMEM)
    in_hbm = pl.BlockSpec(memory_space=pltpu.HBM)
    hbm = lambda x: pltpu.with_memory_space_constraint(x, pltpu.HBM)
    sums_type = jax.ShapeDtypeStruct((3, rows, tile), F32)
    places = panels * slots + 1
    cost = pl.CostEstimate(flops=3_000_000_000, bytes_accessed=8_000_000, transcendentals=0)
    coef_type = jax.ShapeDtypeStruct((places, rows, width), BF16)
    left_shape = (panels, slots, tile, width)
    coef_h, coef_l, right_kept, left_kept, other = pl.pallas_call(
        adjoint_kernel,
        in_specs=[in_smem] + [in_hbm] * 4,
        out_specs=[in_vmem] * 5,
        out_shape=[
            coef_type,
            coef_type,
            jax.ShapeDtypeStruct((places, tile, 2 * width), BF16),
            jax.ShapeDtypeStruct(left_shape, F32),
            sums_type,
        ],
        scratch_shapes=[
            pltpu.SMEM(tile_src.shape, jnp.int32),
            pltpu.VMEM((panels, 2, virtual, tile), F32),
            pltpu.VMEM((panels, slots, tile, width), F32),
            pltpu.SemaphoreType.DMA((4, panels)),
        ],
        compiler_params=pltpu.CompilerParams(vmem_limit_bytes=28 * mib),
        name="adjoint",
    )(me, hbm(tile_src), hbm(wavefield[0]), hbm(left), hbm(right))
    def local(kernel, outs, *args, scalars=True, limit=4):
        return pl.pallas_call(
            kernel,
            in_specs=[in_smem] * (2 * scalars) + [in_vmem] * (len(args) - 2 * scalars),
            out_specs=[in_vmem] * len(outs),
            out_shape=[jax.ShapeDtypeStruct(shape, dtype) for shape, dtype in outs],
            compiler_params=pltpu.CompilerParams(vmem_limit_bytes=limit * mib),
            cost_estimate=cost if scalars else None,
            name=kernel.__name__,
        )(*args)

    swap = [(i, i ^ 1) for i in range(8)]

    def exchange(x):
        return lax.ppermute(x, "panel", swap)

    def shift(x, by):
        return lax.ppermute(x, "panel", [(i, (i + 2 * by) % 8) for i in range(8)])

    half = rows // 2
    swapped = exchange(other)
    (own,) = local(own_kernel, [((3, rows, tile), F32)], tile_src, me, coef_h, coef_l, right_kept, limit=16)
    up, down, up_half, down_half = local(
        chip_sum_kernel, [((2, half, tile), F32)] * 2 + [((half, tile), F32)] * 2, own, swapped, scalars=False
    )
    below, above = shift(up, 1), shift(down, -1)
    after = exchange(up[0, :8, :width])
    here, left_h, left_l = local(
        here_kernel,
        [((2, rows, tile), F32), (left_shape, BF16), (left_shape, BF16)],
        tile_src, me, coef_h, coef_l, right_kept, left_kept, after, limit=20,
    )
    swapped = exchange(here[0])
    below, above, swapped = lax.optimization_barrier((below, above, swapped))
    up, down = local(relay_kernel, [((half, tile), F32)] * 2, up_half, below, down_half, above, scalars=False)
    (moved,) = local(
        sum_kernel,
        [((count, 4 * group, tile // 2), F32)],
        here, swapped, below, above, shift(up, 1), shift(down, -1), scalars=False,
    )
    moved = lax.all_to_all(moved, "freq", split_axis=0, concat_axis=0, tiled=True)

    into, outof = time_tables(count)
    (gated,) = local(
        gate_kernel,
        [((2 * rows, tile // 2), F32)],
        tile_src, me, moved.reshape(2 * rows, tile // 2), onset, jnp.asarray(into), jnp.asarray(outof), limit=12,
    )
    back = lax.all_to_all(gated.reshape(count, 4 * group, tile // 2), "freq", split_axis=0, concat_axis=0, tiled=True)

    def forward(steps, tiles, total, last=False):
        number = len(tiles)
        return pl.pallas_call(
            functools.partial(forward_kernel, steps, last, number // (2 * len(steps))),
            in_specs=[in_smem, in_smem] + [in_vmem] * (number + 4),
            out_specs=in_hbm if last else in_vmem,
            out_shape=jax.ShapeDtypeStruct(total.shape, F32),
            scratch_shapes=[pltpu.VMEM((panels, 2, virtual, tile), F32), pltpu.SemaphoreType.DMA((panels,))] if last else [],
            compiler_params=pltpu.CompilerParams(vmem_limit_bytes=24 * mib),
            cost_estimate=cost,
            name="forward_" + "_".join(str(step) for step in steps),
        )(tile_src, me, *tiles, left_h, left_l, right_kept, total)

    above, below = shift(back, -1), shift(back, 1)
    total = forward((0,), [back, exchange(back)], direct[0])
    above, below, total = lax.optimization_barrier((above, below, total))
    cut = count // 2
    far = [shift(above[:cut], -1), shift(below[cut:], 1)]
    above_other, below_other = exchange(above), exchange(below)
    total = forward((1,), [above, above_other], total)
    *far, total = lax.optimization_barrier((*far, total))
    far = far + [exchange(part) for part in far]
    total = forward((3,), [below, below_other], total)
    return forward((2,), far, total, last=True)[None]


def solution(mesh):
    in_specs = (
        P("freq", None, None, "panel"),
        P("freq", None, None, "panel"),
        P("freq", "panel", None, None),
        P("freq", "panel", None, None, None),
        P("panel", None),
        P("freq", None),
    )
    out_specs = P("freq", None, None, "panel")
    return jax.shard_map(shards, mesh=mesh, in_specs=in_specs, out_specs=out_specs, check_vma=False)
```

```python
import functools
import math

import jax
import jax.numpy as jnp
import ml_dtypes
import numpy as np
from jax import lax
from jax.experimental import pallas as pl
from jax.experimental.pallas import tpu as pltpu
from jax.sharding import PartitionSpec as P

NT = 1024
FIRST_BIN = 8
T_USED = 896

F32 = jnp.float32
BF16 = jnp.bfloat16
NN = (((1,), (0,)), ((), ()))
NT_DIMS = (((1,), (1,)), ((), ()))
AWAY = (2, 1, 3)


def split(x):
    high = x.astype(BF16)
    low = (x - high.astype(F32)).astype(BF16)
    return high, low


def dot(a, b, dims=NN):
    return lax.dot_general(a, b, dims, preferred_element_type=F32)


def pair_coef(products, rank):
    half = products.shape[0] // 2
    real, imag = products[:half], products[half:]
    lane = lax.broadcasted_iota(jnp.int32, real.shape, 1)
    sign = jnp.where(lane < rank, 1.0, -1.0).astype(F32)
    first = real + sign * pltpu.roll(imag, rank, 1)
    second = imag - sign * pltpu.roll(real, rank, 1)
    return jnp.concatenate([first, second], axis=0)


def find_slot(src_ref, panel, target, slots):
    slot, found = jnp.int32(0), jnp.int32(0)
    for s in range(slots):
        hit = src_ref[panel, s] == target
        slot = jnp.where(hit, s, slot)
        found = jnp.where(hit, 1, found)
    return slot, jnp.where(found > 0, panel * slots + slot, src_ref.shape[0] * slots)


def tile_of(me, step, other):
    return lax.rem(me // 2 + step, 4) * 2 + lax.rem(me + other, 2)


def spread(src_ref, me, targets, coef_h, coef_l, right_ref, out_ref):
    width = coef_h.shape[2]
    for i, (step, other) in enumerate(targets):
        target = tile_of(me, step, other)
        parts = []
        for p in range(src_ref.shape[0]):
            _, at = find_slot(src_ref, p, target, src_ref.shape[1])
            parts.append((coef_h[at], coef_l[at], right_ref[at, :, :width], right_ref[at, :, width:]))
        high, low, right_h, right_l = (jnp.concatenate(x, axis=1) for x in zip(*parts))
        out_ref[i] = dot(high, right_h, NT_DIMS) + dot(low, right_h, NT_DIMS) + dot(high, right_l, NT_DIMS)


def adjoint_kernel(
    me_ref, src_hbm, field_hbm, left_hbm, right_hbm,
    coef_h, coef_l, right_ref, left_ref, out_ref,
    src_ref, field_ref, raw_ref, sems,
):
    panels, slots, tile, width = left_ref.shape
    copies = []
    for p in range(panels):
        at = pl.ds(p * tile, tile)
        copies.append(
            (
                pltpu.make_async_copy(field_hbm.at[:, :, at], field_ref.at[p], sems.at[0, p]),
                pltpu.make_async_copy(left_hbm.at[:, at, :], left_ref.at[p], sems.at[1, p]),
            )
        )
    rights = [pltpu.make_async_copy(right_hbm.at[p], raw_ref.at[p], sems.at[2, p]) for p in range(panels)]
    names = pltpu.make_async_copy(src_hbm, src_ref, sems.at[3, 0])
    for pair in copies:
        pair[0].start()
        pair[1].start()
    for copy in rights:
        copy.start()
    names.start()
    last = panels * slots
    coef_h[last] = jnp.zeros(coef_h.shape[1:], BF16)
    coef_l[last] = jnp.zeros(coef_l.shape[1:], BF16)
    right_ref[last] = jnp.zeros(right_ref.shape[1:], BF16)
    for p in range(panels):
        copies[p][0].wait()
        copies[p][1].wait()
        field_h, field_l = split(field_ref[p].reshape(-1, tile))
        for s in range(0, slots, 2):
            left_h, left_l = split(jnp.concatenate([left_ref[p, s], left_ref[p, s + 1]], axis=1))
            both = dot(field_h, left_h) + dot(field_l, left_h) + dot(field_h, left_l)
            for k in range(2):
                high, low = split(pair_coef(both[:, k * width : (k + 1) * width], width // 2))
                coef_h[p * slots + s + k] = high
                coef_l[p * slots + s + k] = low
    for p in range(panels):
        rights[p].wait()
        for s in range(slots):
            right_ref[p * slots + s] = jnp.concatenate(split(raw_ref[p, s]), axis=1)
    names.wait()
    spread(src_ref, me_ref[0], [(step, 1) for step in AWAY], coef_h, coef_l, right_ref, out_ref)


def own_kernel(src_ref, me_ref, coef_h, coef_l, right_ref, out_ref):
    spread(src_ref, me_ref[0], [(step, 0) for step in AWAY], coef_h, coef_l, right_ref, out_ref)


def here_kernel(src_ref, me_ref, coef_h, coef_l, right_ref, left_ref, _, out_ref, left_h, left_l):
    spread(src_ref, me_ref[0], [(0, 1), (0, 0)], coef_h, coef_l, right_ref, out_ref)
    for p in range(left_ref.shape[0]):
        for s in range(left_ref.shape[1]):
            left_h[p, s], left_l[p, s] = split(left_ref[p, s])


def chip_sum_kernel(own_ref, swapped_ref, up_ref, down_ref, up_half, down_half):
    half = up_half.shape[0]
    up_ref[0] = own_ref[0, :half] + swapped_ref[0, :half]
    down_ref[0] = own_ref[0, half:] + swapped_ref[0, half:]
    up_half[...] = own_ref[1, :half] + swapped_ref[1, :half]
    up_ref[1] = own_ref[1, half:] + swapped_ref[1, half:]
    down_ref[1] = own_ref[2, :half] + swapped_ref[2, :half]
    down_half[...] = own_ref[2, half:] + swapped_ref[2, half:]


def relay_kernel(up_half, from_below, down_half, from_above, up_ref, down_ref):
    up_ref[...] = up_half[...] + from_below[0]
    down_ref[...] = down_half[...] + from_above[0]


def sum_kernel(here_ref, swapped_ref, below, above, relayed_below, relayed_above, out_ref):
    totals = (
        (here_ref[1, : relayed_below.shape[0]] + swapped_ref[: relayed_below.shape[0]])
        + (relayed_below[...] + above[1]),
        (here_ref[1, relayed_below.shape[0] :] + swapped_ref[relayed_below.shape[0] :])
        + (relayed_above[...] + below[1]),
    )
    for c, total in enumerate(totals):
        rows, cols = total.shape
        lanes = cols // 2
        block = total.reshape(rows // 8, 8, cols)
        left, right = block[:, :, :lanes], block[:, :, lanes:]
        low = lax.broadcasted_iota(jnp.int32, left.shape, 1) < 4
        even = jnp.where(low, left, pltpu.roll(right, 4, 1))
        odd = jnp.where(low, pltpu.roll(left, 4, 1), right)
        out_ref[:, 8 * c : 8 * c + 8, :] = jnp.stack([even, odd], axis=1).reshape(rows // 4, 8, lanes)


def gate_kernel(me_ref, x_ref, onset_ref, into_ref, outof_ref, y_ref):
    group = onset_ref.shape[0]
    lanes = x_ref.shape[1]
    bands = outof_ref.shape[0] // 2
    for v in range(group):
        picks = [pl.ds(h * group + v, bands, stride=2 * group) for h in range(2)]
        high, low = split(jnp.concatenate([x_ref[pick, :] for pick in picks], axis=1))
        traces = dot(into_ref[...], jnp.concatenate([high, high, low], axis=0))
        when = lax.broadcasted_iota(jnp.int32, traces.shape, 0)
        gated = jnp.where(when < onset_ref[v : v + 1, :], traces, 0.0)
        high, low = split(gated)
        pair = dot(outof_ref[...], high)
        back = pair[:bands] + pair[bands:] + dot(outof_ref[:bands, :], low)
        for h in range(2):
            y_ref[picks[h], :] = back[:, h * lanes : (h + 1) * lanes]


def forward_kernel(steps, last, pieces, src_ref, me_ref, *refs):
    number = 2 * len(steps)
    left_h, left_l, right_ref, total_ref, out_ref, *scratch = refs[number * pieces :]
    panels, slots, tile, width = left_h.shape
    me = me_ref[0]
    tiles = []
    for i in range(number):
        got = jnp.concatenate([ref[...] for ref in refs[i * pieces : (i + 1) * pieces]], axis=0)
        count, _, lanes = got.shape
        block = got.reshape(count // 2, 2, 2, 8, lanes)
        parts = []
        for c in range(2):
            even, odd = block[:, 0, c], block[:, 1, c]
            low = lax.broadcasted_iota(jnp.int32, even.shape, 1) < 4
            first = jnp.where(low, even, pltpu.roll(odd, 4, 1)).reshape(count * 4, lanes)
            second = jnp.where(low, pltpu.roll(even, 4, 1), odd).reshape(count * 4, lanes)
            parts.append(jnp.concatenate([first, second], axis=1))
        tiles.append(split(jnp.concatenate(parts, axis=0)))
    found = []
    for p in range(panels):
        parts = []
        for i, (high, low) in enumerate(tiles):
            slot, place = find_slot(src_ref, p, tile_of(me, steps[i // 2], i % 2), slots)
            right = right_ref[place]
            pair = dot(high, right)
            products = pair[:, :width] + pair[:, width:] + dot(low, right[:, :width])
            parts.append(split(pair_coef(products, width // 2)) + (left_h[p, slot], left_l[p, slot]))
        found.append(parts)
    copies = []
    for p in range(panels):
        at = slice(p * tile, (p + 1) * tile)
        high, low, there_h, there_l = (jnp.concatenate(x, axis=1) for x in zip(*found[p]))
        result = dot(high, there_h, NT_DIMS) + dot(low, there_h, NT_DIMS) + dot(high, there_l, NT_DIMS)
        result = total_ref[:, :, at] - result.reshape(total_ref.shape[0], total_ref.shape[1], tile)
        if last:
            kept, sems = scratch
            kept[p] = result
            copies.append(pltpu.make_async_copy(kept.at[p], out_ref.at[:, :, pl.ds(p * tile, tile)], sems.at[p]))
            copies[p].start()
        else:
            out_ref[:, :, at] = result
    for copy in copies:
        copy.wait()


def time_tables(count):
    times = np.arange(T_USED, dtype=np.int64)
    phase = (np.arange(count, dtype=np.int64) + FIRST_BIN)[None, :] * times[:, None] % NT
    angle = 2.0 * math.pi / NT * phase
    waves = np.stack([np.cos(angle), -np.sin(angle)], axis=2).reshape(T_USED, 2 * count)

    def parts(x):
        high = x.astype(ml_dtypes.bfloat16)
        return high, (x - high.astype(np.float64)).astype(ml_dtypes.bfloat16)

    high, low = parts(waves / math.sqrt(count))
    into = np.concatenate([high, low, high], axis=1)
    high, low = parts(waves.T / math.sqrt(NT))
    return into, np.concatenate([high, low], axis=0)


def shards(wavefield, direct, left_factors, right_factors, tile_src, onset):
    panels, slots = tile_src.shape
    tile, width = right_factors.shape[3:]
    virtual = wavefield.shape[2]
    rows = 2 * virtual
    mib = 1024 * 1024
    left = jnp.transpose(left_factors[0], (1, 0, 2))
    right = right_factors[0]
    me = lax.axis_index("panel").astype(jnp.int32)[None]
    count = lax.axis_size("freq")
    group = virtual // count

    in_vmem = pl.BlockSpec(memory_space=pltpu.VMEM)
    in_smem = pl.BlockSpec(memory_space=pltpu.SMEM)
    in_hbm = pl.BlockSpec(memory_space=pltpu.HBM)
    hbm = lambda x: pltpu.with_memory_space_constraint(x, pltpu.HBM)
    sums_type = jax.ShapeDtypeStruct((3, rows, tile), F32)
    places = panels * slots + 1
    cost = pl.CostEstimate(flops=3_000_000_000, bytes_accessed=8_000_000, transcendentals=0)
    coef_type = jax.ShapeDtypeStruct((places, rows, width), BF16)
    left_shape = (panels, slots, tile, width)
    coef_h, coef_l, right_kept, left_kept, other = pl.pallas_call(
        adjoint_kernel,
        in_specs=[in_smem] + [in_hbm] * 4,
        out_specs=[in_vmem] * 5,
        out_shape=[
            coef_type,
            coef_type,
            jax.ShapeDtypeStruct((places, tile, 2 * width), BF16),
            jax.ShapeDtypeStruct(left_shape, F32),
            sums_type,
        ],
        scratch_shapes=[
            pltpu.SMEM(tile_src.shape, jnp.int32),
            pltpu.VMEM((panels, 2, virtual, tile), F32),
            pltpu.VMEM((panels, slots, tile, width), F32),
            pltpu.SemaphoreType.DMA((4, panels)),
        ],
        compiler_params=pltpu.CompilerParams(vmem_limit_bytes=28 * mib),
        name="adjoint",
    )(me, hbm(tile_src), hbm(wavefield[0]), hbm(left), hbm(right))
    def local(kernel, outs, *args, scalars=True, limit=4):
        return pl.pallas_call(
            kernel,
            in_specs=[in_smem] * (2 * scalars) + [in_vmem] * (len(args) - 2 * scalars),
            out_specs=[in_vmem] * len(outs),
            out_shape=[jax.ShapeDtypeStruct(shape, dtype) for shape, dtype in outs],
            compiler_params=pltpu.CompilerParams(vmem_limit_bytes=limit * mib),
            cost_estimate=cost if scalars else None,
            name=kernel.__name__,
        )(*args)

    swap = [(i, i ^ 1) for i in range(8)]

    def exchange(x):
        return lax.ppermute(x, "panel", swap)

    def shift(x, by):
        return lax.ppermute(x, "panel", [(i, (i + 2 * by) % 8) for i in range(8)])

    half = rows // 2
    swapped = exchange(other)
    (own,) = local(own_kernel, [((3, rows, tile), F32)], tile_src, me, coef_h, coef_l, right_kept, limit=16)
    up, down, up_half, down_half = local(
        chip_sum_kernel, [((2, half, tile), F32)] * 2 + [((half, tile), F32)] * 2, own, swapped, scalars=False
    )
    below, above = shift(up, 1), shift(down, -1)
    after = exchange(up[0, :8, :width])
    here, left_h, left_l = local(
        here_kernel,
        [((2, rows, tile), F32), (left_shape, BF16), (left_shape, BF16)],
        tile_src, me, coef_h, coef_l, right_kept, left_kept, after, limit=20,
    )
    swapped = exchange(here[0])
    below, above, swapped = lax.optimization_barrier((below, above, swapped))
    up, down = local(relay_kernel, [((half, tile), F32)] * 2, up_half, below, down_half, above, scalars=False)
    (moved,) = local(
        sum_kernel,
        [((count, 4 * group, tile // 2), F32)],
        here, swapped, below, above, shift(up, 1), shift(down, -1), scalars=False,
    )
    moved = lax.all_to_all(moved, "freq", split_axis=0, concat_axis=0, tiled=True)

    into, outof = time_tables(count)
    whole = lambda shape: pl.BlockSpec(shape, lambda i, *_: (0,) * len(shape))
    gated = pl.pallas_call(
        gate_kernel,
        grid_spec=pltpu.PrefetchScalarGridSpec(
            num_scalar_prefetch=1,
            grid=(1,),
            in_specs=[
                whole((2 * rows, tile // 2)),
                pl.BlockSpec((group, tile), lambda i, me_ref: (0, me_ref[0])),
                whole(into.shape),
                whole(outof.shape),
            ],
            out_specs=whole((2 * rows, tile // 2)),
        ),
        out_shape=jax.ShapeDtypeStruct((2 * rows, tile // 2), F32),
        compiler_params=pltpu.CompilerParams(vmem_limit_bytes=12 * mib),
        name="gate",
    )(me, moved.reshape(2 * rows, tile // 2), onset, jnp.asarray(into), jnp.asarray(outof))
    back = lax.all_to_all(gated.reshape(count, 4 * group, tile // 2), "freq", split_axis=0, concat_axis=0, tiled=True)

    def forward(steps, tiles, total, last=False):
        number = len(tiles)
        return pl.pallas_call(
            functools.partial(forward_kernel, steps, last, number // (2 * len(steps))),
            in_specs=[in_smem, in_smem] + [in_vmem] * (number + 4),
            out_specs=in_hbm if last else in_vmem,
            out_shape=jax.ShapeDtypeStruct(total.shape, F32),
            scratch_shapes=[pltpu.VMEM((panels, 2, virtual, tile), F32), pltpu.SemaphoreType.DMA((panels,))] if last else [],
            compiler_params=pltpu.CompilerParams(vmem_limit_bytes=24 * mib),
            cost_estimate=cost,
            name="forward_" + "_".join(str(step) for step in steps),
        )(tile_src, me, *tiles, left_h, left_l, right_kept, total)

    above, below = shift(back, -1), shift(back, 1)
    total = forward((0,), [back, exchange(back)], direct[0])
    above, below, total = lax.optimization_barrier((above, below, total))
    cut = count // 2
    far = [shift(above[:cut], -1), shift(below[cut:], 1)]
    above_other, below_other = exchange(above), exchange(below)
    total = forward((1,), [above, above_other], total)
    *far, total = lax.optimization_barrier((*far, total))
    far = far + [exchange(part) for part in far]
    total = forward((3,), [below, below_other], total)
    return forward((2,), far, total, last=True)[None]


def solution(mesh):
    in_specs = (
        P("freq", None, None, "panel"),
        P("freq", None, None, "panel"),
        P("freq", "panel", None, None),
        P("freq", "panel", None, None, None),
        P("panel", None),
        P("freq", None),
    )
    out_specs = P("freq", None, None, "panel")
    return jax.shard_map(shards, mesh=mesh, in_specs=in_specs, out_specs=out_specs, check_vma=False)
```

```python
import functools
import math

import jax
import jax.numpy as jnp
import ml_dtypes
import numpy as np
from jax import lax
from jax.experimental import pallas as pl
from jax.experimental.pallas import tpu as pltpu
from jax.sharding import PartitionSpec as P

NT = 1024
FIRST_BIN = 8
T_USED = 896

F32 = jnp.float32
BF16 = jnp.bfloat16
NN = (((1,), (0,)), ((), ()))
NT_DIMS = (((1,), (1,)), ((), ()))
AWAY = (2, 1, 3)


def split(x):
    high = x.astype(BF16)
    low = (x - high.astype(F32)).astype(BF16)
    return high, low


def dot(a, b, dims=NN):
    return lax.dot_general(a, b, dims, preferred_element_type=F32)


def pair_coef(products, rank):
    half = products.shape[0] // 2
    real, imag = products[:half], products[half:]
    lane = lax.broadcasted_iota(jnp.int32, real.shape, 1)
    sign = jnp.where(lane < rank, 1.0, -1.0).astype(F32)
    first = real + sign * pltpu.roll(imag, rank, 1)
    second = imag - sign * pltpu.roll(real, rank, 1)
    return jnp.concatenate([first, second], axis=0)


def find_slot(src_ref, panel, target, slots):
    slot, found = jnp.int32(0), jnp.int32(0)
    for s in range(slots):
        hit = src_ref[panel, s] == target
        slot = jnp.where(hit, s, slot)
        found = jnp.where(hit, 1, found)
    return slot, jnp.where(found > 0, panel * slots + slot, src_ref.shape[0] * slots)


def tile_of(me, step, other):
    return lax.rem(me // 2 + step, 4) * 2 + lax.rem(me + other, 2)


def spread(src_ref, me, targets, coef_h, coef_l, right_ref, out_ref):
    width = coef_h.shape[2]
    for i, (step, other) in enumerate(targets):
        target = tile_of(me, step, other)
        parts = []
        for p in range(src_ref.shape[0]):
            _, at = find_slot(src_ref, p, target, src_ref.shape[1])
            parts.append((coef_h[at], coef_l[at], right_ref[at, :, :width], right_ref[at, :, width:]))
        high, low, right_h, right_l = (jnp.concatenate(x, axis=1) for x in zip(*parts))
        out_ref[i] = dot(high, right_h, NT_DIMS) + dot(low, right_h, NT_DIMS) + dot(high, right_l, NT_DIMS)


def adjoint_kernel(
    me_ref, src_hbm, field_hbm, left_hbm, right_hbm,
    coef_h, coef_l, right_ref, left_ref, out_ref,
    src_ref, field_ref, raw_ref, sems,
):
    panels, slots, tile, width = left_ref.shape
    copies = []
    for p in range(panels):
        at = pl.ds(p * tile, tile)
        copies.append(
            (
                pltpu.make_async_copy(field_hbm.at[:, :, at], field_ref.at[p], sems.at[0, p]),
                pltpu.make_async_copy(left_hbm.at[:, at, :], left_ref.at[p], sems.at[1, p]),
            )
        )
    rights = [pltpu.make_async_copy(right_hbm.at[p], raw_ref.at[p], sems.at[2, p]) for p in range(panels)]
    names = pltpu.make_async_copy(src_hbm, src_ref, sems.at[3, 0])
    for pair in copies:
        pair[0].start()
        pair[1].start()
    for copy in rights:
        copy.start()
    names.start()
    last = panels * slots
    coef_h[last] = jnp.zeros(coef_h.shape[1:], BF16)
    coef_l[last] = jnp.zeros(coef_l.shape[1:], BF16)
    right_ref[last] = jnp.zeros(right_ref.shape[1:], BF16)
    for p in range(panels):
        copies[p][0].wait()
        copies[p][1].wait()
        field_h, field_l = split(field_ref[p].reshape(-1, tile))
        for s in range(0, slots, 2):
            left_h, left_l = split(jnp.concatenate([left_ref[p, s], left_ref[p, s + 1]], axis=1))
            both = dot(field_h, left_h) + dot(field_l, left_h) + dot(field_h, left_l)
            for k in range(2):
                high, low = split(pair_coef(both[:, k * width : (k + 1) * width], width // 2))
                coef_h[p * slots + s + k] = high
                coef_l[p * slots + s + k] = low
    for p in range(panels):
        rights[p].wait()
        for s in range(slots):
            right_ref[p * slots + s] = jnp.concatenate(split(raw_ref[p, s]), axis=1)
    names.wait()
    spread(src_ref, me_ref[0], [(step, 1) for step in AWAY], coef_h, coef_l, right_ref, out_ref)


def own_kernel(src_ref, me_ref, coef_h, coef_l, right_ref, out_ref):
    spread(src_ref, me_ref[0], [(step, 0) for step in AWAY], coef_h, coef_l, right_ref, out_ref)


def here_kernel(src_ref, me_ref, coef_h, coef_l, right_ref, left_ref, _, out_ref, left_h, left_l):
    spread(src_ref, me_ref[0], [(0, 1), (0, 0)], coef_h, coef_l, right_ref, out_ref)
    for p in range(left_ref.shape[0]):
        for s in range(left_ref.shape[1]):
            left_h[p, s], left_l[p, s] = split(left_ref[p, s])


def chip_sum_kernel(own_ref, swapped_ref, up_ref, down_ref, up_half, down_half):
    half = up_half.shape[0]
    up_ref[0] = own_ref[0, :half] + swapped_ref[0, :half]
    down_ref[0] = own_ref[0, half:] + swapped_ref[0, half:]
    up_half[...] = own_ref[1, :half] + swapped_ref[1, :half]
    up_ref[1] = own_ref[1, half:] + swapped_ref[1, half:]
    down_ref[1] = own_ref[2, :half] + swapped_ref[2, :half]
    down_half[...] = own_ref[2, half:] + swapped_ref[2, half:]


def relay_kernel(up_half, from_below, down_half, from_above, up_ref, down_ref):
    up_ref[...] = up_half[...] + from_below[0]
    down_ref[...] = down_half[...] + from_above[0]


def sum_kernel(here_ref, swapped_ref, below, above, relayed_below, relayed_above, out_ref):
    totals = (
        (here_ref[1, : relayed_below.shape[0]] + swapped_ref[: relayed_below.shape[0]])
        + (relayed_below[...] + above[1]),
        (here_ref[1, relayed_below.shape[0] :] + swapped_ref[relayed_below.shape[0] :])
        + (relayed_above[...] + below[1]),
    )
    for c, total in enumerate(totals):
        rows, cols = total.shape
        lanes = cols // 2
        block = total.reshape(rows // 8, 8, cols)
        left, right = block[:, :, :lanes], block[:, :, lanes:]
        low = lax.broadcasted_iota(jnp.int32, left.shape, 1) < 4
        even = jnp.where(low, left, pltpu.roll(right, 4, 1))
        odd = jnp.where(low, pltpu.roll(left, 4, 1), right)
        out_ref[:, 8 * c : 8 * c + 8, :] = jnp.stack([even, odd], axis=1).reshape(rows // 4, 8, lanes)


def gate_kernel(me_ref, x_ref, onset_ref, into_ref, outof_ref, y_ref):
    group = onset_ref.shape[0]
    lanes = x_ref.shape[1]
    bands = outof_ref.shape[0] // 2
    for v in range(group):
        picks = [pl.ds(h * group + v, bands, stride=2 * group) for h in range(2)]
        high, low = split(jnp.concatenate([x_ref[pick, :] for pick in picks], axis=1))
        traces = dot(into_ref[...], jnp.concatenate([high, high, low], axis=0))
        when = lax.broadcasted_iota(jnp.int32, traces.shape, 0)
        gated = jnp.where(when < onset_ref[v : v + 1, :], traces, 0.0)
        high, low = split(gated)
        pair = dot(outof_ref[...], high)
        back = pair[:bands] + pair[bands:] + dot(outof_ref[:bands, :], low)
        for h in range(2):
            y_ref[picks[h], :] = back[:, h * lanes : (h + 1) * lanes]


def forward_kernel(steps, last, pieces, src_ref, me_ref, *refs):
    number = 2 * len(steps)
    left_h, left_l, right_ref, total_ref, out_ref, *scratch = refs[number * pieces :]
    panels, slots, tile, width = left_h.shape
    me = me_ref[0]
    tiles = []
    for i in range(number):
        got = jnp.concatenate([ref[...] for ref in refs[i * pieces : (i + 1) * pieces]], axis=0)
        count, _, lanes = got.shape
        block = got.reshape(count // 2, 2, 2, 8, lanes)
        parts = []
        for c in range(2):
            even, odd = block[:, 0, c], block[:, 1, c]
            low = lax.broadcasted_iota(jnp.int32, even.shape, 1) < 4
            first = jnp.where(low, even, pltpu.roll(odd, 4, 1)).reshape(count * 4, lanes)
            second = jnp.where(low, pltpu.roll(even, 4, 1), odd).reshape(count * 4, lanes)
            parts.append(jnp.concatenate([first, second], axis=1))
        tiles.append(split(jnp.concatenate(parts, axis=0)))
    found = []
    for p in range(panels):
        parts = []
        for i, (high, low) in enumerate(tiles):
            slot, place = find_slot(src_ref, p, tile_of(me, steps[i // 2], i % 2), slots)
            right = right_ref[place]
            pair = dot(high, right)
            products = pair[:, :width] + pair[:, width:] + dot(low, right[:, :width])
            parts.append(split(pair_coef(products, width // 2)) + (left_h[p, slot], left_l[p, slot]))
        found.append(parts)
    copies = []
    for p in range(panels):
        at = slice(p * tile, (p + 1) * tile)
        high, low, there_h, there_l = (jnp.concatenate(x, axis=1) for x in zip(*found[p]))
        result = dot(high, there_h, NT_DIMS) + dot(low, there_h, NT_DIMS) + dot(high, there_l, NT_DIMS)
        result = total_ref[:, :, at] - result.reshape(total_ref.shape[0], total_ref.shape[1], tile)
        if last:
            kept, sems = scratch
            kept[p] = result
            copies.append(pltpu.make_async_copy(kept.at[p], out_ref.at[:, :, pl.ds(p * tile, tile)], sems.at[p]))
            copies[p].start()
        else:
            out_ref[:, :, at] = result
    for copy in copies:
        copy.wait()


def time_tables(count):
    times = np.arange(T_USED, dtype=np.int64)
    phase = (np.arange(count, dtype=np.int64) + FIRST_BIN)[None, :] * times[:, None] % NT
    angle = 2.0 * math.pi / NT * phase
    waves = np.stack([np.cos(angle), -np.sin(angle)], axis=2).reshape(T_USED, 2 * count)

    def parts(x):
        high = x.astype(ml_dtypes.bfloat16)
        return high, (x - high.astype(np.float64)).astype(ml_dtypes.bfloat16)

    high, low = parts(waves / math.sqrt(count))
    into = np.concatenate([high, low, high], axis=1)
    high, low = parts(waves.T / math.sqrt(NT))
    return into, np.concatenate([high, low], axis=0)


def shards(wavefield, direct, left_factors, right_factors, tile_src, onset):
    panels, slots = tile_src.shape
    tile, width = right_factors.shape[3:]
    virtual = wavefield.shape[2]
    rows = 2 * virtual
    mib = 1024 * 1024
    left = jnp.transpose(left_factors[0], (1, 0, 2))
    right = right_factors[0]
    me = lax.axis_index("panel").astype(jnp.int32)[None]
    count = lax.axis_size("freq")
    group = virtual // count

    in_vmem = pl.BlockSpec(memory_space=pltpu.VMEM)
    in_smem = pl.BlockSpec(memory_space=pltpu.SMEM)
    in_hbm = pl.BlockSpec(memory_space=pltpu.HBM)
    hbm = lambda x: pltpu.with_memory_space_constraint(x, pltpu.HBM)
    sums_type = jax.ShapeDtypeStruct((3, rows, tile), F32)
    places = panels * slots + 1
    cost = pl.CostEstimate(flops=3_000_000_000, bytes_accessed=8_000_000, transcendentals=0)
    coef_type = jax.ShapeDtypeStruct((places, rows, width), BF16)
    left_shape = (panels, slots, tile, width)
    coef_h, coef_l, right_kept, left_kept, other = pl.pallas_call(
        adjoint_kernel,
        in_specs=[in_smem] + [in_hbm] * 4,
        out_specs=[in_vmem] * 5,
        out_shape=[
            coef_type,
            coef_type,
            jax.ShapeDtypeStruct((places, tile, 2 * width), BF16),
            jax.ShapeDtypeStruct(left_shape, F32),
            sums_type,
        ],
        scratch_shapes=[
            pltpu.SMEM(tile_src.shape, jnp.int32),
            pltpu.VMEM((panels, 2, virtual, tile), F32),
            pltpu.VMEM((panels, slots, tile, width), F32),
            pltpu.SemaphoreType.DMA((4, panels)),
        ],
        compiler_params=pltpu.CompilerParams(vmem_limit_bytes=28 * mib),
        name="adjoint",
    )(me, hbm(tile_src), hbm(wavefield[0]), hbm(left), hbm(right))
    def local(kernel, outs, *args, scalars=True, limit=4):
        return pl.pallas_call(
            kernel,
            in_specs=[in_smem] * (2 * scalars) + [in_vmem] * (len(args) - 2 * scalars),
            out_specs=[in_vmem] * len(outs),
            out_shape=[jax.ShapeDtypeStruct(shape, dtype) for shape, dtype in outs],
            compiler_params=pltpu.CompilerParams(vmem_limit_bytes=limit * mib),
            cost_estimate=cost if scalars else None,
            name=kernel.__name__,
        )(*args)

    swap = [(i, i ^ 1) for i in range(8)]

    def exchange(x):
        return lax.ppermute(x, "panel", swap)

    def shift(x, by):
        return lax.ppermute(x, "panel", [(i, (i + 2 * by) % 8) for i in range(8)])

    half = rows // 2
    swapped = exchange(other)
    (own,) = local(own_kernel, [((3, rows, tile), F32)], tile_src, me, coef_h, coef_l, right_kept, limit=16)
    up, down, up_half, down_half = local(
        chip_sum_kernel, [((2, half, tile), F32)] * 2 + [((half, tile), F32)] * 2, own, swapped, scalars=False
    )
    below, above = shift(up, 1), shift(down, -1)
    after = exchange(up[0, :8, :width])
    here, left_h, left_l = local(
        here_kernel,
        [((2, rows, tile), F32), (left_shape, BF16), (left_shape, BF16)],
        tile_src, me, coef_h, coef_l, right_kept, left_kept, after, limit=20,
    )
    swapped = exchange(here[0])
    below, above, swapped = lax.optimization_barrier((below, above, swapped))
    up, down = local(relay_kernel, [((half, tile), F32)] * 2, up_half, below, down_half, above, scalars=False)
    (moved,) = local(
        sum_kernel,
        [((count, 4 * group, tile // 2), F32)],
        here, swapped, below, above, shift(up, 1), shift(down, -1), scalars=False,
    )
    moved = lax.all_to_all(moved, "freq", split_axis=0, concat_axis=0, tiled=True)

    into, outof = time_tables(count)
    whole = lambda shape: pl.BlockSpec(shape, lambda i, *_: (0,) * len(shape))
    gated = pl.pallas_call(
        gate_kernel,
        grid_spec=pltpu.PrefetchScalarGridSpec(
            num_scalar_prefetch=1,
            grid=(1,),
            in_specs=[
                whole((2 * rows, tile // 2)),
                pl.BlockSpec((group, tile), lambda i, me_ref: (0, me_ref[0])),
                whole(into.shape),
                whole(outof.shape),
            ],
            out_specs=whole((2 * rows, tile // 2)),
        ),
        out_shape=jax.ShapeDtypeStruct((2 * rows, tile // 2), F32),
        compiler_params=pltpu.CompilerParams(vmem_limit_bytes=12 * mib),
        name="gate",
    )(me, moved.reshape(2 * rows, tile // 2), onset, jnp.asarray(into), jnp.asarray(outof))
    back = lax.all_to_all(gated.reshape(count, 4 * group, tile // 2), "freq", split_axis=0, concat_axis=0, tiled=True)

    def forward(steps, tiles, total, last=False):
        number = len(tiles)
        return pl.pallas_call(
            functools.partial(forward_kernel, steps, last, number // (2 * len(steps))),
            in_specs=[in_smem, in_smem] + [in_vmem] * (number + 4),
            out_specs=in_hbm if last else in_vmem,
            out_shape=jax.ShapeDtypeStruct(total.shape, F32),
            scratch_shapes=[pltpu.VMEM((panels, 2, virtual, tile), F32), pltpu.SemaphoreType.DMA((panels,))] if last else [],
            compiler_params=pltpu.CompilerParams(vmem_limit_bytes=24 * mib),
            cost_estimate=cost,
            name="forward_" + "_".join(str(step) for step in steps),
        )(tile_src, me, *tiles, left_h, left_l, right_kept, total)

    there = [shift(back, -step) for step in (1, 3, 2)]
    total = forward((0,), [back, exchange(back)], direct[0])
    *there, total = lax.optimization_barrier((*there, total))
    for step, mine in zip((1, 3, 2), there):
        total = forward((step,), [mine, exchange(mine)], total, last=step == 2)
    return total[None]


def solution(mesh):
    in_specs = (
        P("freq", None, None, "panel"),
        P("freq", None, None, "panel"),
        P("freq", "panel", None, None),
        P("freq", "panel", None, None, None),
        P("panel", None),
        P("freq", None),
    )
    out_specs = P("freq", None, None, "panel")
    return jax.shard_map(shards, mesh=mesh, in_specs=in_specs, out_specs=out_specs, check_vma=False)
```

```python
import functools
import math

import jax
import jax.numpy as jnp
import ml_dtypes
import numpy as np
from jax import lax
from jax.experimental import pallas as pl
from jax.experimental.pallas import tpu as pltpu
from jax.sharding import PartitionSpec as P

NT = 1024
FIRST_BIN = 8
T_USED = 896

F32 = jnp.float32
BF16 = jnp.bfloat16
NN = (((1,), (0,)), ((), ()))
NT_DIMS = (((1,), (1,)), ((), ()))
FAR, NEAR = (2,), (1, 3)


def split(x):
    high = x.astype(BF16)
    low = (x - high.astype(F32)).astype(BF16)
    return high, low


def dot(a, b, dims=NN):
    return lax.dot_general(a, b, dims, preferred_element_type=F32)


def pair_coef(products, rank):
    half = products.shape[0] // 2
    real, imag = products[:half], products[half:]
    lane = lax.broadcasted_iota(jnp.int32, real.shape, 1)
    sign = jnp.where(lane < rank, 1.0, -1.0).astype(F32)
    first = real + sign * pltpu.roll(imag, rank, 1)
    second = imag - sign * pltpu.roll(real, rank, 1)
    return jnp.concatenate([first, second], axis=0)


def find_slot(src_ref, panel, target, slots):
    slot, found = jnp.int32(0), jnp.int32(0)
    for s in range(slots):
        hit = src_ref[panel, s] == target
        slot = jnp.where(hit, s, slot)
        found = jnp.where(hit, 1, found)
    return slot, jnp.where(found > 0, panel * slots + slot, src_ref.shape[0] * slots)


def tile_of(me, step, other):
    return lax.rem(me // 2 + step, 4) * 2 + lax.rem(me + other, 2)


def spread(src_ref, me, targets, coef_h, coef_l, right_ref, out_ref):
    width = coef_h.shape[2]
    for i, (step, other) in enumerate(targets):
        target = tile_of(me, step, other)
        parts = []
        for p in range(src_ref.shape[0]):
            _, at = find_slot(src_ref, p, target, src_ref.shape[1])
            parts.append((coef_h[at], coef_l[at], right_ref[at, :, :width], right_ref[at, :, width:]))
        high, low, right_h, right_l = (jnp.concatenate(x, axis=1) for x in zip(*parts))
        out_ref[i] = dot(high, right_h, NT_DIMS) + dot(low, right_h, NT_DIMS) + dot(high, right_l, NT_DIMS)


def adjoint_kernel(
    me_ref, src_hbm, field_hbm, left_hbm, right_hbm,
    coef_h, coef_l, right_ref, left_ref, far_ref, near_ref,
    src_ref, field_ref, raw_ref, sems,
):
    panels, slots, tile, width = left_ref.shape
    copies = []
    for p in range(panels):
        at = pl.ds(p * tile, tile)
        copies.append(
            (
                pltpu.make_async_copy(field_hbm.at[:, :, at], field_ref.at[p], sems.at[0, p]),
                pltpu.make_async_copy(left_hbm.at[:, at, :], left_ref.at[p], sems.at[1, p]),
            )
        )
    rights = [pltpu.make_async_copy(right_hbm.at[p], raw_ref.at[p], sems.at[2, p]) for p in range(panels)]
    names = pltpu.make_async_copy(src_hbm, src_ref, sems.at[3, 0])
    for pair in copies:
        pair[0].start()
        pair[1].start()
    for copy in rights:
        copy.start()
    names.start()
    last = panels * slots
    coef_h[last] = jnp.zeros(coef_h.shape[1:], BF16)
    coef_l[last] = jnp.zeros(coef_l.shape[1:], BF16)
    right_ref[last] = jnp.zeros(right_ref.shape[1:], BF16)
    for p in range(panels):
        copies[p][0].wait()
        copies[p][1].wait()
        field_h, field_l = split(field_ref[p].reshape(-1, tile))
        for s in range(0, slots, 2):
            left_h, left_l = split(jnp.concatenate([left_ref[p, s], left_ref[p, s + 1]], axis=1))
            both = dot(field_h, left_h) + dot(field_l, left_h) + dot(field_h, left_l)
            for k in range(2):
                high, low = split(pair_coef(both[:, k * width : (k + 1) * width], width // 2))
                coef_h[p * slots + s + k] = high
                coef_l[p * slots + s + k] = low
    for p in range(panels):
        rights[p].wait()
        for s in range(slots):
            right_ref[p * slots + s] = jnp.concatenate(split(raw_ref[p, s]), axis=1)
    names.wait()
    spread(src_ref, me_ref[0], [(step, 1) for step in FAR], coef_h, coef_l, right_ref, far_ref)
    spread(src_ref, me_ref[0], [(step, 1) for step in NEAR], coef_h, coef_l, right_ref, near_ref)


def far_kernel(src_ref, me_ref, coef_h, coef_l, right_ref, out_ref):
    spread(src_ref, me_ref[0], [(step, 0) for step in FAR], coef_h, coef_l, right_ref, out_ref)


def near_kernel(src_ref, me_ref, coef_h, coef_l, right_ref, _, out_ref):
    spread(src_ref, me_ref[0], [(step, 0) for step in NEAR], coef_h, coef_l, right_ref, out_ref)


def here_kernel(src_ref, me_ref, coef_h, coef_l, right_ref, left_ref, _, out_ref, left_h, left_l):
    spread(src_ref, me_ref[0], [(0, 1), (0, 0)], coef_h, coef_l, right_ref, out_ref)
    for p in range(left_ref.shape[0]):
        for s in range(left_ref.shape[1]):
            left_h[p, s], left_l[p, s] = split(left_ref[p, s])


def far_sum_kernel(own_ref, swapped_ref, up_ref, down_ref):
    half = up_ref.shape[0]
    up_ref[...] = own_ref[0, :half] + swapped_ref[0, :half]
    down_ref[...] = own_ref[0, half:] + swapped_ref[0, half:]


def near_sum_kernel(own_ref, swapped_ref, from_below, from_above, up_ref, down_ref):
    half = from_below.shape[0]
    up_ref[:half] = (own_ref[0, :half] + swapped_ref[0, :half]) + from_below[...]
    up_ref[half:] = own_ref[0, half:] + swapped_ref[0, half:]
    down_ref[:half] = own_ref[1, :half] + swapped_ref[1, :half]
    down_ref[half:] = (own_ref[1, half:] + swapped_ref[1, half:]) + from_above[...]


def sum_kernel(here_ref, swapped_ref, below, above, out_ref):
    all_parts = (here_ref[1] + swapped_ref[...]) + (below[...] + above[...])
    half = all_parts.shape[0] // 2
    totals = (all_parts[:half], all_parts[half:])
    for c, total in enumerate(totals):
        rows, cols = total.shape
        lanes = cols // 2
        block = total.reshape(rows // 8, 8, cols)
        left, right = block[:, :, :lanes], block[:, :, lanes:]
        low = lax.broadcasted_iota(jnp.int32, left.shape, 1) < 4
        even = jnp.where(low, left, pltpu.roll(right, 4, 1))
        odd = jnp.where(low, pltpu.roll(left, 4, 1), right)
        out_ref[:, 8 * c : 8 * c + 8, :] = jnp.stack([even, odd], axis=1).reshape(rows // 4, 8, lanes)


def gate_kernel(me_ref, x_ref, onset_ref, into_ref, outof_ref, y_ref):
    group = onset_ref.shape[0]
    lanes = x_ref.shape[1]
    bands = outof_ref.shape[0] // 2
    for v in range(group):
        picks = [pl.ds(h * group + v, bands, stride=2 * group) for h in range(2)]
        high, low = split(jnp.concatenate([x_ref[pick, :] for pick in picks], axis=1))
        traces = dot(into_ref[...], jnp.concatenate([high, high, low], axis=0))
        when = lax.broadcasted_iota(jnp.int32, traces.shape, 0)
        gated = jnp.where(when < onset_ref[v : v + 1, :], traces, 0.0)
        high, low = split(gated)
        pair = dot(outof_ref[...], high)
        back = pair[:bands] + pair[bands:] + dot(outof_ref[:bands, :], low)
        for h in range(2):
            y_ref[picks[h], :] = back[:, h * lanes : (h + 1) * lanes]


def forward_kernel(steps, last, pieces, src_ref, me_ref, *refs):
    number = 2 * len(steps)
    left_h, left_l, right_ref, total_ref, out_ref, *scratch = refs[number * pieces :]
    panels, slots, tile, width = left_h.shape
    me = me_ref[0]
    tiles = []
    for i in range(number):
        got = jnp.concatenate([ref[...] for ref in refs[i * pieces : (i + 1) * pieces]], axis=0)
        count, _, lanes = got.shape
        block = got.reshape(count // 2, 2, 2, 8, lanes)
        parts = []
        for c in range(2):
            even, odd = block[:, 0, c], block[:, 1, c]
            low = lax.broadcasted_iota(jnp.int32, even.shape, 1) < 4
            first = jnp.where(low, even, pltpu.roll(odd, 4, 1)).reshape(count * 4, lanes)
            second = jnp.where(low, pltpu.roll(even, 4, 1), odd).reshape(count * 4, lanes)
            parts.append(jnp.concatenate([first, second], axis=1))
        tiles.append(split(jnp.concatenate(parts, axis=0)))
    found = []
    for p in range(panels):
        parts = []
        for i, (high, low) in enumerate(tiles):
            slot, place = find_slot(src_ref, p, tile_of(me, steps[i // 2], i % 2), slots)
            right = right_ref[place]
            pair = dot(high, right)
            products = pair[:, :width] + pair[:, width:] + dot(low, right[:, :width])
            parts.append(split(pair_coef(products, width // 2)) + (left_h[p, slot], left_l[p, slot]))
        found.append(parts)
    copies = []
    for p in range(panels):
        at = slice(p * tile, (p + 1) * tile)
        high, low, there_h, there_l = (jnp.concatenate(x, axis=1) for x in zip(*found[p]))
        result = dot(high, there_h, NT_DIMS) + dot(low, there_h, NT_DIMS) + dot(high, there_l, NT_DIMS)
        result = total_ref[:, :, at] - result.reshape(total_ref.shape[0], total_ref.shape[1], tile)
        if last:
            kept, sems = scratch
            kept[p] = result
            copies.append(pltpu.make_async_copy(kept.at[p], out_ref.at[:, :, pl.ds(p * tile, tile)], sems.at[p]))
            copies[p].start()
        else:
            out_ref[:, :, at] = result
    for copy in copies:
        copy.wait()


def time_tables(count):
    times = np.arange(T_USED, dtype=np.int64)
    phase = (np.arange(count, dtype=np.int64) + FIRST_BIN)[None, :] * times[:, None] % NT
    angle = 2.0 * math.pi / NT * phase
    waves = np.stack([np.cos(angle), -np.sin(angle)], axis=2).reshape(T_USED, 2 * count)

    def parts(x):
        high = x.astype(ml_dtypes.bfloat16)
        return high, (x - high.astype(np.float64)).astype(ml_dtypes.bfloat16)

    high, low = parts(waves / math.sqrt(count))
    into = np.concatenate([high, low, high], axis=1)
    high, low = parts(waves.T / math.sqrt(NT))
    return into, np.concatenate([high, low], axis=0)


def shards(wavefield, direct, left_factors, right_factors, tile_src, onset):
    panels, slots = tile_src.shape
    tile, width = right_factors.shape[3:]
    virtual = wavefield.shape[2]
    rows = 2 * virtual
    mib = 1024 * 1024
    left = jnp.transpose(left_factors[0], (1, 0, 2))
    right = right_factors[0]
    me = lax.axis_index("panel").astype(jnp.int32)[None]
    count = lax.axis_size("freq")
    group = virtual // count

    in_vmem = pl.BlockSpec(memory_space=pltpu.VMEM)
    in_smem = pl.BlockSpec(memory_space=pltpu.SMEM)
    in_hbm = pl.BlockSpec(memory_space=pltpu.HBM)
    hbm = lambda x: pltpu.with_memory_space_constraint(x, pltpu.HBM)
    places = panels * slots + 1
    cost = pl.CostEstimate(flops=3_000_000_000, bytes_accessed=8_000_000, transcendentals=0)
    coef_type = jax.ShapeDtypeStruct((places, rows, width), BF16)
    left_shape = (panels, slots, tile, width)
    coef_h, coef_l, right_kept, left_kept, far, near = pl.pallas_call(
        adjoint_kernel,
        in_specs=[in_smem] + [in_hbm] * 4,
        out_specs=[in_vmem] * 6,
        out_shape=[
            coef_type,
            coef_type,
            jax.ShapeDtypeStruct((places, tile, 2 * width), BF16),
            jax.ShapeDtypeStruct(left_shape, F32),
            jax.ShapeDtypeStruct((len(FAR), rows, tile), F32),
            jax.ShapeDtypeStruct((len(NEAR), rows, tile), F32),
        ],
        scratch_shapes=[
            pltpu.SMEM(tile_src.shape, jnp.int32),
            pltpu.VMEM((panels, 2, virtual, tile), F32),
            pltpu.VMEM((panels, slots, tile, width), F32),
            pltpu.SemaphoreType.DMA((4, panels)),
        ],
        compiler_params=pltpu.CompilerParams(vmem_limit_bytes=28 * mib),
        name="adjoint",
    )(me, hbm(tile_src), hbm(wavefield[0]), hbm(left), hbm(right))
    def local(kernel, outs, *args, scalars=True, limit=4, cost=None):
        return pl.pallas_call(
            kernel,
            in_specs=[in_smem] * (2 * scalars) + [in_vmem] * (len(args) - 2 * scalars),
            out_specs=[in_vmem] * len(outs),
            out_shape=[jax.ShapeDtypeStruct(shape, dtype) for shape, dtype in outs],
            compiler_params=pltpu.CompilerParams(vmem_limit_bytes=limit * mib),
            cost_estimate=cost,
            name=kernel.__name__,
        )(*args)

    swap = [(i, i ^ 1) for i in range(8)]

    def exchange(x):
        return lax.ppermute(x, "panel", swap)

    def shift(x, by):
        return lax.ppermute(x, "panel", [(i, (i + 2 * by) % 8) for i in range(8)])

    half = rows // 2
    factors = (tile_src, me, coef_h, coef_l, right_kept)
    one, two = [((1, rows, tile), F32)], [((2, rows, tile), F32)]
    swapped_far, swapped = exchange(far), exchange(near)
    (far,) = local(far_kernel, one, *factors, limit=16, cost=cost)
    up, down = local(far_sum_kernel, [((half, tile), F32)] * 2, far, swapped_far, scalars=False)
    below, above = shift(up, 1), shift(down, -1)
    after = exchange(up[:8, :width])
    (near,) = local(near_kernel, two, *factors, after, limit=16, cost=cost)
    up, down = local(near_sum_kernel, [((rows, tile), F32)] * 2, near, swapped, below, above, scalars=False)
    below, above = shift(up, 1), shift(down, -1)
    after = exchange(up[:8, :width])
    here, left_h, left_l = local(
        here_kernel, two + [(left_shape, BF16), (left_shape, BF16)], *factors, left_kept, after, limit=20, cost=cost
    )
    (moved,) = local(
        sum_kernel, [((count, 4 * group, tile // 2), F32)], here, exchange(here[0]), below, above, scalars=False
    )
    moved = lax.all_to_all(moved, "freq", split_axis=0, concat_axis=0, tiled=True)

    into, outof = time_tables(count)
    whole = lambda shape: pl.BlockSpec(shape, lambda i, *_: (0,) * len(shape))
    gated = pl.pallas_call(
        gate_kernel,
        grid_spec=pltpu.PrefetchScalarGridSpec(
            num_scalar_prefetch=1,
            grid=(1,),
            in_specs=[
                whole((2 * rows, tile // 2)),
                pl.BlockSpec((group, tile), lambda i, me_ref: (0, me_ref[0])),
                whole(into.shape),
                whole(outof.shape),
            ],
            out_specs=whole((2 * rows, tile // 2)),
        ),
        out_shape=jax.ShapeDtypeStruct((2 * rows, tile // 2), F32),
        compiler_params=pltpu.CompilerParams(vmem_limit_bytes=12 * mib),
        name="gate",
    )(me, moved.reshape(2 * rows, tile // 2), onset, jnp.asarray(into), jnp.asarray(outof))
    back = lax.all_to_all(gated.reshape(count, 4 * group, tile // 2), "freq", split_axis=0, concat_axis=0, tiled=True)

    def forward(steps, tiles, total, last=False):
        number = len(tiles)
        return pl.pallas_call(
            functools.partial(forward_kernel, steps, last, number // (2 * len(steps))),
            in_specs=[in_smem, in_smem] + [in_vmem] * (number + 4),
            out_specs=in_hbm if last else in_vmem,
            out_shape=jax.ShapeDtypeStruct(total.shape, F32),
            scratch_shapes=[pltpu.VMEM((panels, 2, virtual, tile), F32), pltpu.SemaphoreType.DMA((panels,))] if last else [],
            compiler_params=pltpu.CompilerParams(vmem_limit_bytes=24 * mib),
            cost_estimate=cost,
            name="forward_" + "_".join(str(step) for step in steps),
        )(tile_src, me, *tiles, left_h, left_l, right_kept, total)

    above, below = shift(back, -1), shift(back, 1)
    total = forward((0,), [back, exchange(back)], direct[0])
    above, below, total = lax.optimization_barrier((above, below, total))
    cut = count // 2
    far = [shift(above[:cut], -1), shift(below[cut:], 1)]
    above_other, below_other = exchange(above), exchange(below)
    total = forward((1,), [above, above_other], total)
    *far, total = lax.optimization_barrier((*far, total))
    far = far + [exchange(part) for part in far]
    total = forward((3,), [below, below_other], total)
    return forward((2,), far, total, last=True)[None]


def solution(mesh):
    in_specs = (
        P("freq", None, None, "panel"),
        P("freq", None, None, "panel"),
        P("freq", "panel", None, None),
        P("freq", "panel", None, None, None),
        P("panel", None),
        P("freq", None),
    )
    out_specs = P("freq", None, None, "panel")
    return jax.shard_map(shards, mesh=mesh, in_specs=in_specs, out_specs=out_specs, check_vma=False)
```

```python
import functools
import math

import jax
import jax.numpy as jnp
import ml_dtypes
import numpy as np
from jax import lax
from jax.experimental import pallas as pl
from jax.experimental.pallas import tpu as pltpu
from jax.sharding import PartitionSpec as P

NT = 1024
FIRST_BIN = 8
T_USED = 896

F32 = jnp.float32
BF16 = jnp.bfloat16
NN = (((1,), (0,)), ((), ()))
NT_DIMS = (((1,), (1,)), ((), ()))
AWAY = (2, 1, 3)


def split(x):
    high = x.astype(BF16)
    low = (x - high.astype(F32)).astype(BF16)
    return high, low


def dot(a, b, dims=NN):
    return lax.dot_general(a, b, dims, preferred_element_type=F32)


def pair_coef(products, rank):
    half = products.shape[0] // 2
    real, imag = products[:half], products[half:]
    lane = lax.broadcasted_iota(jnp.int32, real.shape, 1)
    sign = jnp.where(lane < rank, 1.0, -1.0).astype(F32)
    first = real + sign * pltpu.roll(imag, rank, 1)
    second = imag - sign * pltpu.roll(real, rank, 1)
    return jnp.concatenate([first, second], axis=0)


def find_slot(src_ref, panel, target, slots):
    slot, found = jnp.int32(0), jnp.int32(0)
    for s in range(slots):
        hit = src_ref[panel, s] == target
        slot = jnp.where(hit, s, slot)
        found = jnp.where(hit, 1, found)
    return slot, jnp.where(found > 0, panel * slots + slot, src_ref.shape[0] * slots)


def tile_of(me, step, other):
    return lax.rem(me // 2 + step, 4) * 2 + lax.rem(me + other, 2)


def spread(src_ref, me, targets, coef_h, coef_l, right_ref, out_ref):
    width = coef_h.shape[2]
    for i, (step, other) in enumerate(targets):
        target = tile_of(me, step, other)
        parts = []
        for p in range(src_ref.shape[0]):
            _, at = find_slot(src_ref, p, target, src_ref.shape[1])
            parts.append((coef_h[at], coef_l[at], right_ref[at, :, :width], right_ref[at, :, width:]))
        high, low, right_h, right_l = (jnp.concatenate(x, axis=1) for x in zip(*parts))
        out_ref[i] = dot(high, right_h, NT_DIMS) + dot(low, right_h, NT_DIMS) + dot(high, right_l, NT_DIMS)


def adjoint_kernel(
    me_ref, src_hbm, field_hbm, left_hbm, right_hbm,
    coef_h, coef_l, right_ref, left_ref, out_ref,
    src_ref, field_ref, raw_ref, sems,
):
    panels, slots, tile, width = left_ref.shape
    copies = []
    for p in range(panels):
        at = pl.ds(p * tile, tile)
        copies.append(
            (
                pltpu.make_async_copy(field_hbm.at[:, :, at], field_ref.at[p], sems.at[0, p]),
                pltpu.make_async_copy(left_hbm.at[:, at, :], left_ref.at[p], sems.at[1, p]),
            )
        )
    rights = [pltpu.make_async_copy(right_hbm.at[p], raw_ref.at[p], sems.at[2, p]) for p in range(panels)]
    names = pltpu.make_async_copy(src_hbm, src_ref, sems.at[3, 0])
    for pair in copies:
        pair[0].start()
        pair[1].start()
    for copy in rights:
        copy.start()
    names.start()
    last = panels * slots
    coef_h[last] = jnp.zeros(coef_h.shape[1:], BF16)
    coef_l[last] = jnp.zeros(coef_l.shape[1:], BF16)
    right_ref[last] = jnp.zeros(right_ref.shape[1:], BF16)
    for p in range(panels):
        copies[p][0].wait()
        copies[p][1].wait()
        field_h, field_l = split(field_ref[p].reshape(-1, tile))
        for s in range(0, slots, 2):
            left_h, left_l = split(jnp.concatenate([left_ref[p, s], left_ref[p, s + 1]], axis=1))
            both = dot(field_h, left_h) + dot(field_l, left_h) + dot(field_h, left_l)
            for k in range(2):
                high, low = split(pair_coef(both[:, k * width : (k + 1) * width], width // 2))
                coef_h[p * slots + s + k] = high
                coef_l[p * slots + s + k] = low
    for p in range(panels):
        rights[p].wait()
        for s in range(slots):
            right_ref[p * slots + s] = jnp.concatenate(split(raw_ref[p, s]), axis=1)
    names.wait()
    spread(src_ref, me_ref[0], [(step, 1) for step in AWAY], coef_h, coef_l, right_ref, out_ref)


def own_kernel(src_ref, me_ref, coef_h, coef_l, right_ref, out_ref):
    spread(src_ref, me_ref[0], [(step, 0) for step in AWAY], coef_h, coef_l, right_ref, out_ref)


def here_kernel(src_ref, me_ref, coef_h, coef_l, right_ref, left_ref, _, out_ref, left_h, left_l):
    spread(src_ref, me_ref[0], [(0, 1), (0, 0)], coef_h, coef_l, right_ref, out_ref)
    for p in range(left_ref.shape[0]):
        for s in range(left_ref.shape[1]):
            left_h[p, s], left_l[p, s] = split(left_ref[p, s])


def chip_sum_kernel(own_ref, swapped_ref, up_ref, down_ref, up_half, down_half):
    half = up_half.shape[0]
    up_ref[0] = own_ref[0, :half] + swapped_ref[0, :half]
    down_ref[0] = own_ref[0, half:] + swapped_ref[0, half:]
    up_half[...] = own_ref[1, :half] + swapped_ref[1, :half]
    up_ref[1] = own_ref[1, half:] + swapped_ref[1, half:]
    down_ref[1] = own_ref[2, :half] + swapped_ref[2, :half]
    down_half[...] = own_ref[2, half:] + swapped_ref[2, half:]


def relay_kernel(up_half, from_below, down_half, from_above, up_ref, down_ref):
    up_ref[...] = up_half[...] + from_below[0]
    down_ref[...] = down_half[...] + from_above[0]


def sum_kernel(here_ref, swapped_ref, below, above, relayed_below, relayed_above, out_ref):
    totals = (
        (here_ref[1, : relayed_below.shape[0]] + swapped_ref[: relayed_below.shape[0]])
        + (relayed_below[...] + above[1]),
        (here_ref[1, relayed_below.shape[0] :] + swapped_ref[relayed_below.shape[0] :])
        + (relayed_above[...] + below[1]),
    )
    for c, total in enumerate(totals):
        rows, cols = total.shape
        lanes = cols // 2
        block = total.reshape(rows // 8, 8, cols)
        left, right = block[:, :, :lanes], block[:, :, lanes:]
        low = lax.broadcasted_iota(jnp.int32, left.shape, 1) < 4
        even = jnp.where(low, left, pltpu.roll(right, 4, 1))
        odd = jnp.where(low, pltpu.roll(left, 4, 1), right)
        out_ref[:, 8 * c : 8 * c + 8, :] = jnp.stack([even, odd], axis=1).reshape(rows // 4, 8, lanes)


def gate_kernel(me_ref, x_ref, onset_ref, into_ref, outof_ref, y_ref):
    group = onset_ref.shape[0]
    lanes = x_ref.shape[1]
    bands = outof_ref.shape[0] // 2
    for v in range(group):
        picks = [pl.ds(h * group + v, bands, stride=2 * group) for h in range(2)]
        high, low = split(jnp.concatenate([x_ref[pick, :] for pick in picks], axis=1))
        traces = dot(into_ref[...], jnp.concatenate([high, high, low], axis=0))
        when = lax.broadcasted_iota(jnp.int32, traces.shape, 0)
        gated = jnp.where(when < onset_ref[v : v + 1, :], traces, 0.0)
        high, low = split(gated)
        pair = dot(outof_ref[...], high)
        back = pair[:bands] + pair[bands:] + dot(outof_ref[:bands, :], low)
        for h in range(2):
            y_ref[picks[h], :] = back[:, h * lanes : (h + 1) * lanes]


def forward_kernel(targets, last, pieces, src_ref, me_ref, *refs):
    number = len(targets)
    left_h, left_l, right_ref, total_ref, out_ref, *scratch = refs[number * pieces :]
    panels, slots, tile, width = left_h.shape
    me = me_ref[0]
    tiles = []
    for i in range(number):
        got = jnp.concatenate([ref[...] for ref in refs[i * pieces : (i + 1) * pieces]], axis=0)
        count, _, lanes = got.shape
        block = got.reshape(count // 2, 2, 2, 8, lanes)
        parts = []
        for c in range(2):
            even, odd = block[:, 0, c], block[:, 1, c]
            low = lax.broadcasted_iota(jnp.int32, even.shape, 1) < 4
            first = jnp.where(low, even, pltpu.roll(odd, 4, 1)).reshape(count * 4, lanes)
            second = jnp.where(low, pltpu.roll(even, 4, 1), odd).reshape(count * 4, lanes)
            parts.append(jnp.concatenate([first, second], axis=1))
        tiles.append(split(jnp.concatenate(parts, axis=0)))
    found = []
    for p in range(panels):
        parts = []
        for i, (high, low) in enumerate(tiles):
            slot, place = find_slot(src_ref, p, tile_of(me, *targets[i]), slots)
            right = right_ref[place]
            pair = dot(high, right)
            products = pair[:, :width] + pair[:, width:] + dot(low, right[:, :width])
            parts.append(split(pair_coef(products, width // 2)) + (left_h[p, slot], left_l[p, slot]))
        found.append(parts)
    copies = []
    for p in range(panels):
        at = slice(p * tile, (p + 1) * tile)
        high, low, there_h, there_l = (jnp.concatenate(x, axis=1) for x in zip(*found[p]))
        result = dot(high, there_h, NT_DIMS) + dot(low, there_h, NT_DIMS) + dot(high, there_l, NT_DIMS)
        result = total_ref[:, :, at] - result.reshape(total_ref.shape[0], total_ref.shape[1], tile)
        if last:
            kept, sems = scratch
            kept[p] = result
            copies.append(pltpu.make_async_copy(kept.at[p], out_ref.at[:, :, pl.ds(p * tile, tile)], sems.at[p]))
            copies[p].start()
        else:
            out_ref[:, :, at] = result
    for copy in copies:
        copy.wait()


def time_tables(count):
    times = np.arange(T_USED, dtype=np.int64)
    phase = (np.arange(count, dtype=np.int64) + FIRST_BIN)[None, :] * times[:, None] % NT
    angle = 2.0 * math.pi / NT * phase
    waves = np.stack([np.cos(angle), -np.sin(angle)], axis=2).reshape(T_USED, 2 * count)

    def parts(x):
        high = x.astype(ml_dtypes.bfloat16)
        return high, (x - high.astype(np.float64)).astype(ml_dtypes.bfloat16)

    high, low = parts(waves / math.sqrt(count))
    into = np.concatenate([high, low, high], axis=1)
    high, low = parts(waves.T / math.sqrt(NT))
    return into, np.concatenate([high, low], axis=0)


def shards(wavefield, direct, left_factors, right_factors, tile_src, onset):
    panels, slots = tile_src.shape
    tile, width = right_factors.shape[3:]
    virtual = wavefield.shape[2]
    rows = 2 * virtual
    mib = 1024 * 1024
    left = jnp.transpose(left_factors[0], (1, 0, 2))
    right = right_factors[0]
    me = lax.axis_index("panel").astype(jnp.int32)[None]
    count = lax.axis_size("freq")
    group = virtual // count

    in_vmem = pl.BlockSpec(memory_space=pltpu.VMEM)
    in_smem = pl.BlockSpec(memory_space=pltpu.SMEM)
    in_hbm = pl.BlockSpec(memory_space=pltpu.HBM)
    hbm = lambda x: pltpu.with_memory_space_constraint(x, pltpu.HBM)
    sums_type = jax.ShapeDtypeStruct((3, rows, tile), F32)
    places = panels * slots + 1
    cost = pl.CostEstimate(flops=3_000_000_000, bytes_accessed=8_000_000, transcendentals=0)
    coef_type = jax.ShapeDtypeStruct((places, rows, width), BF16)
    left_shape = (panels, slots, tile, width)
    coef_h, coef_l, right_kept, left_kept, other = pl.pallas_call(
        adjoint_kernel,
        in_specs=[in_smem] + [in_hbm] * 4,
        out_specs=[in_vmem] * 5,
        out_shape=[
            coef_type,
            coef_type,
            jax.ShapeDtypeStruct((places, tile, 2 * width), BF16),
            jax.ShapeDtypeStruct(left_shape, F32),
            sums_type,
        ],
        scratch_shapes=[
            pltpu.SMEM(tile_src.shape, jnp.int32),
            pltpu.VMEM((panels, 2, virtual, tile), F32),
            pltpu.VMEM((panels, slots, tile, width), F32),
            pltpu.SemaphoreType.DMA((4, panels)),
        ],
        compiler_params=pltpu.CompilerParams(vmem_limit_bytes=28 * mib),
        name="adjoint",
    )(me, hbm(tile_src), hbm(wavefield[0]), hbm(left), hbm(right))
    def local(kernel, outs, *args, scalars=True, limit=4):
        return pl.pallas_call(
            kernel,
            in_specs=[in_smem] * (2 * scalars) + [in_vmem] * (len(args) - 2 * scalars),
            out_specs=[in_vmem] * len(outs),
            out_shape=[jax.ShapeDtypeStruct(shape, dtype) for shape, dtype in outs],
            compiler_params=pltpu.CompilerParams(vmem_limit_bytes=limit * mib),
            cost_estimate=cost if scalars else None,
            name=kernel.__name__,
        )(*args)

    swap = [(i, i ^ 1) for i in range(8)]

    def exchange(x):
        return lax.ppermute(x, "panel", swap)

    def shift(x, by):
        return lax.ppermute(x, "panel", [(i, (i + 2 * by) % 8) for i in range(8)])

    half = rows // 2
    swapped = exchange(other)
    (own,) = local(own_kernel, [((3, rows, tile), F32)], tile_src, me, coef_h, coef_l, right_kept, limit=16)
    up, down, up_half, down_half = local(
        chip_sum_kernel, [((2, half, tile), F32)] * 2 + [((half, tile), F32)] * 2, own, swapped, scalars=False
    )
    below, above = shift(up, 1), shift(down, -1)
    after = exchange(up[0, :8, :width])
    here, left_h, left_l = local(
        here_kernel,
        [((2, rows, tile), F32), (left_shape, BF16), (left_shape, BF16)],
        tile_src, me, coef_h, coef_l, right_kept, left_kept, after, limit=20,
    )
    swapped = exchange(here[0])
    below, above, swapped = lax.optimization_barrier((below, above, swapped))
    up, down = local(relay_kernel, [((half, tile), F32)] * 2, up_half, below, down_half, above, scalars=False)
    (moved,) = local(
        sum_kernel,
        [((count, 4 * group, tile // 2), F32)],
        here, swapped, below, above, shift(up, 1), shift(down, -1), scalars=False,
    )
    moved = lax.all_to_all(moved, "freq", split_axis=0, concat_axis=0, tiled=True)

    into, outof = time_tables(count)
    whole = lambda shape: pl.BlockSpec(shape, lambda i, *_: (0,) * len(shape))
    gated = pl.pallas_call(
        gate_kernel,
        grid_spec=pltpu.PrefetchScalarGridSpec(
            num_scalar_prefetch=1,
            grid=(1,),
            in_specs=[
                whole((2 * rows, tile // 2)),
                pl.BlockSpec((group, tile), lambda i, me_ref: (0, me_ref[0])),
                whole(into.shape),
                whole(outof.shape),
            ],
            out_specs=whole((2 * rows, tile // 2)),
        ),
        out_shape=jax.ShapeDtypeStruct((2 * rows, tile // 2), F32),
        compiler_params=pltpu.CompilerParams(vmem_limit_bytes=12 * mib),
        name="gate",
    )(me, moved.reshape(2 * rows, tile // 2), onset, jnp.asarray(into), jnp.asarray(outof))
    back = lax.all_to_all(gated.reshape(count, 4 * group, tile // 2), "freq", split_axis=0, concat_axis=0, tiled=True)

    def forward(targets, tiles, total, last=False):
        number = len(tiles)
        return pl.pallas_call(
            functools.partial(forward_kernel, targets, last, number // len(targets)),
            in_specs=[in_smem, in_smem] + [in_vmem] * (number + 4),
            out_specs=in_hbm if last else in_vmem,
            out_shape=jax.ShapeDtypeStruct(total.shape, F32),
            scratch_shapes=[pltpu.VMEM((panels, 2, virtual, tile), F32), pltpu.SemaphoreType.DMA((panels,))] if last else [],
            compiler_params=pltpu.CompilerParams(vmem_limit_bytes=24 * mib),
            cost_estimate=cost,
            name="forward_" + "_".join(f"{step}{other}" for step, other in targets),
        )(tile_src, me, *tiles, left_h, left_l, right_kept, total)

    above, below = shift(back, -1), shift(back, 1)
    both = lambda step: ((step, 0), (step, 1))
    total = forward(both(0), [back, exchange(back)], direct[0])
    above, below, total = lax.optimization_barrier((above, below, total))
    cut = count // 2
    far = [shift(above[:cut], -1), shift(below[cut:], 1)]
    above_other, below_other = exchange(above), exchange(below)
    total = forward(both(1), [above, above_other], total)
    total = forward(both(3), [below, below_other], total)
    *far, total = lax.optimization_barrier((*far, total))
    far_other = [exchange(part) for part in far]
    total = forward(((2, 0),), far, total)
    return forward(((2, 1),), far_other, total, last=True)[None]


def solution(mesh):
    in_specs = (
        P("freq", None, None, "panel"),
        P("freq", None, None, "panel"),
        P("freq", "panel", None, None),
        P("freq", "panel", None, None, None),
        P("panel", None),
        P("freq", None),
    )
    out_specs = P("freq", None, None, "panel")
    return jax.shard_map(shards, mesh=mesh, in_specs=in_specs, out_specs=out_specs, check_vma=False)
```
